512 devices in a mesh: row: 16 (over y, z_hi), col: 32 (over z_lo, x, core).
Axes of the slice: x: 4, y: 4, z: 16 (z_hi: 4, z_lo: 4; z = z_hi * 4 + z_lo), core: 2. Of those that a mesh axis runs over, the one named last changes fastest.
Arguments:
- normals: float32 [12288, 12288], P('row', 'col'), may hold values from -1 to 4, as said below
- design: float32 [512, 12288], P('row', 'col'), may hold values from -0.25 to 0.25
- filter_blocks: float32 [2, 32, 32], replicated, may hold values from -4 to 4, as said below
- regular: float32 [12288], replicated, may hold values from 0.1 to 1
Outputs:
- factored: float32 [12288, 12288], P('row', 'col')
The draws below stay inside these ranges and needn't reach their ends.
Inputs may be any that keep to these rules, and one draw needn't show every extreme that they name: normals is symmetric; each diagonal entry is at least 1 and each off-diagonal entry has magnitude at most 1 / 256. filter_blocks[0][i, j] = f[i - j] for i >= j and 0 above the diagonal; filter_blocks[1][i, j] = f[32 + i - j] for j >= i and 0 below; f holds the 33 taps of one causal filter with f[0] at least 1.
All inputs are finite; a program needn't handle non-finite values.
Results may differ from the reference program's by a relative error of at most 0.00007.
Values sent between devices are 32-bit elements; how exact they have to be, the bound alone decides.
A program may use at most 64 MiB of HBM per device.

```python
import math
import jax
import jax.numpy as jnp
from jax import lax

M = 12288
B = 256
P_SIZE = 32
OBS = 512


def draw_normals(key, part):
    key_noise = jax.random.fold_in(key, 11)
    key_diag = jax.random.fold_in(key, 12)
    noise = jax.random.uniform(key_noise, (M, M), jnp.float32, -1.0, 1.0)
    symmetric = (noise + noise.T) * (0.5 / B)
    diagonal = jax.random.uniform(key_diag, (M,), jnp.float32, 1.0, 2.0)
    positions = jnp.arange(M, dtype=jnp.int32)
    return jnp.where(positions[:, None] == positions[None, :], diagonal[:, None], symmetric)


def draw_filter_blocks(key, part):
    key_lead = jax.random.fold_in(key, 21)
    key_taps = jax.random.fold_in(key, 22)
    leading = jax.random.uniform(key_lead, (1,), jnp.float32, 1.0, 1.5)
    scales = 0.5 / jnp.sqrt(jnp.arange(1, P_SIZE + 1, dtype=jnp.float32))
    later_taps = jax.random.truncated_normal(key_taps, -6.0, 6.0, (P_SIZE,), jnp.float32) * scales
    filter_taps = jnp.concatenate([leading, later_taps])
    row_pos = jnp.arange(P_SIZE, dtype=jnp.int32)[:, None]
    col_pos = jnp.arange(P_SIZE, dtype=jnp.int32)[None, :]
    lag_own = row_pos - col_pos
    lag_prior = P_SIZE + row_pos - col_pos
    own_block = jnp.where(lag_own >= 0, filter_taps[jnp.clip(lag_own, 0, P_SIZE)], 0.0)
    prior_block = jnp.where(col_pos >= row_pos, filter_taps[jnp.clip(lag_prior, 0, P_SIZE)], 0.0)
    return jnp.stack([own_block, prior_block]).astype(jnp.float32)


def steps_of(own_key, extent, shards, low, top_value):
    def one(dim, parts):
        steps = jax.random.uniform(jax.random.fold_in(jax.random.fold_in(own_key, 6), dim), (parts,), jnp.float32, low / len(shards), top_value / len(shards))
        return jnp.repeat(jnp.exp(steps), extent[dim] // parts).reshape((-1,) + (1,) * (len(extent) - dim - 1))

    factor_of = one(*shards[0])
    for cut in shards[1:]:
        factor_of = factor_of * one(*cut)
    return factor_of


def scatter_about(key, shape, scale, most, split=(), kind=jnp.bfloat16):
    drawn = scale * jax.random.normal(key, shape, jnp.float32)
    if split:
        drawn = drawn * steps_of(key, shape, split, -0.22, 0.18)
    return jnp.clip(drawn, -most, most).astype(kind)


def setup_inputs(seed: int = 0) -> dict:
    arg_keys = jax.random.split(jax.random.key(seed), 5)
    return {
        "normals": draw_normals(jax.random.fold_in(arg_keys[4], 71), 0),
        "design": scatter_about(arg_keys[1], (OBS, M), OBS ** -0.5, 0.25, ((0, 16), (1, 32)), jnp.float32),
        "filter_blocks": draw_filter_blocks(jax.random.fold_in(arg_keys[4], 71), 0),
        "regular": jnp.clip(jnp.exp(jax.random.uniform(arg_keys[3], (M,), jnp.float32, math.log(0.1), math.log(1.0))), 0.1, 1.0),
    }


def reference(normals, design, filter_blocks, regular):
    highest = lax.Precision.HIGHEST
    own_block = filter_blocks[0]
    prior_block = filter_blocks[1]
    blocks = design.reshape(OBS // P_SIZE, P_SIZE, M)
    before = jnp.concatenate([jnp.zeros((1, P_SIZE, M), jnp.float32), blocks[:-1]], axis=0)
    filtered = jnp.einsum('ij,bjc->bic', own_block, blocks, precision=highest)
    filtered = filtered + jnp.einsum('ij,bjc->bic', prior_block, before, precision=highest)
    filtered = filtered.reshape(OBS, M)
    gram_full = jnp.dot(filtered.T.astype(jnp.float32), filtered.astype(jnp.float32), precision=highest, preferred_element_type=jnp.float32)
    positions = jnp.arange(M, dtype=jnp.int32)
    system = (normals + gram_full).at[positions, positions].add(regular)
    corner = system[:B, :B]
    factor = jnp.linalg.cholesky(corner)
    inverse = jax.scipy.linalg.solve_triangular(factor, jnp.eye(B, dtype=jnp.float32), lower=True)
    panel_rows = jnp.dot(system[:, :B].astype(jnp.float32), inverse.T.astype(jnp.float32), precision=highest, preferred_element_type=jnp.float32)
    trailing = system[:, B:] - jnp.dot(panel_rows.astype(jnp.float32), panel_rows[B:].T.astype(jnp.float32), precision=highest, preferred_element_type=jnp.float32)
    return jnp.concatenate([panel_rows, trailing], axis=1)
```

```python
import functools

import jax
import jax.numpy as jnp
from jax import lax
from jax.experimental import pallas as pl
from jax.experimental.pallas import tpu as pltpu
from jax.sharding import PartitionSpec as P

B = 256
P_SIZE = 32
OBS = 512
MESH = pl.DeviceIdType.MESH
VMEM = pltpu.VMEM
HIGHEST = lax.Precision.HIGHEST

DK, D0, NK, N0, DR, NR = range(6)


def comm_kernel(design, normals, dk, dr, d0, nk, nr, n0, ssem, rsem, xsem, psem, qsem, lsem):
    row = lax.axis_index("row")
    col = lax.axis_index("col")
    s = lax.rem(col, 2)
    k = lax.div(col, 2)
    x, zl = lax.rem(k, 4), lax.div(k, 4)
    y, zh = lax.div(row, 4), lax.rem(row, 4)

    def at(y_=None, zh_=None, zl_=None, x_=None, s_=None):
        y_ = y if y_ is None else lax.rem(y_ + 4, 4)
        zh_ = zh if zh_ is None else lax.rem(zh_ + 4, 4)
        zl_ = zl if zl_ is None else lax.rem(zl_ + 4, 4)
        x_ = x if x_ is None else lax.rem(x_ + 4, 4)
        s_ = s if s_ is None else s_
        return (4 * y_ + zh_, 8 * zl_ + 2 * x_ + s_)

    def rslot(y_, zh_):
        return 4 * lax.rem(y_ + 4, 4) + lax.rem(zh_ + 4, 4)

    def kslot(zl_, x_):
        return 4 * lax.rem(zl_ + 4, 4) + lax.rem(x_ + 4, 4)

    flip = (k, 2 * row + s)
    off_diag = k != row
    partner = at(s_=1 - s)

    barrier = pltpu.get_barrier_semaphore()

    def hello(device):
        pl.semaphore_signal(barrier, inc=1, device_id=device, device_id_type=MESH)

    near = [at(zh_=zh + 1), at(zh_=zh - 1), at(y_=y + 1), at(y_=y - 1), at(x_=x + 1), at(x_=x - 1)]
    near += [at(zl_=zl + 1), at(zl_=zl + 2), at(zl_=zl + 3), partner]
    for device in near:
        hello(device)

    @pl.when(off_diag)
    def _():
        hello(flip)

    @pl.when(row != 0)
    def _():
        hello((0, col))

    @pl.when(col != 0)
    def _():
        hello((row, 0))

    bufs = {DK: dk, D0: d0.at[s], NK: nk, N0: n0.at[s], DR: dr.at[s], NR: nr.at[s]}

    own = pltpu.make_async_copy(design, dk.at[row], lsem.at[0])
    own.start()
    own_strip = pltpu.make_async_copy(normals.at[pl.ds(0, 16), :], nk.at[0], lsem.at[1])
    own_corner = pltpu.make_async_copy(design.at[:, pl.ds(0, 128)], d0.at[0, row], lsem.at[2])
    own_flip = pltpu.make_async_copy(design, dr.at[s, k], lsem.at[3])

    @pl.when(row == 0)
    def _():
        own_strip.start()

    @pl.when(col == 0)
    def _():
        own_corner.start()

    @pl.when(k == row)
    def _():
        own_flip.start()

    one = jnp.int32(1)
    count = len(near) + jnp.where(off_diag, one, 0) + jnp.where(row == 0, 15 * one, 0) + jnp.where(col == 0, 31 * one, 0)
    pl.semaphore_wait(barrier, count)

    def send(flow, slot, device, half=None, src=None):
        buf = bufs[flow]
        rows = buf.shape[1]
        if half is None:
            part = buf.at[slot]
        else:
            part = buf.at[slot, pl.ds(half * (rows // 2), rows // 2), :]
        pltpu.make_async_remote_copy(
            src_ref=part if src is None else src,
            dst_ref=part,
            send_sem=ssem.at[flow],
            recv_sem=rsem.at[flow, slot],
            device_id=device,
            device_id_type=MESH,
        ).start()

    def arrived(flow, slot):
        buf = bufs[flow]
        pltpu.make_async_remote_copy(
            src_ref=buf.at[slot],
            dst_ref=buf.at[slot],
            send_sem=ssem.at[flow],
            recv_sem=rsem.at[flow, slot],
            device_id=partner,
            device_id_type=MESH,
        ).wait_recv()

    def other(src, dst, send_sem, recv_sem, device):
        return pltpu.make_async_remote_copy(
            src_ref=src, dst_ref=dst, send_sem=send_sem, recv_sem=recv_sem, device_id=device, device_id_type=MESH
        )

    @pl.when(row == 0)
    def _():
        for t in range(1, 16):
            other(normals.at[pl.ds(16 * t, 16), :], nk.at[t], xsem.at[0], rsem.at[NK, t], (t, col)).start()

    def along_row(flow, source):
        full = d0 if flow == D0 else n0
        for t in range(1, 32):
            h = t % 2
            other(
                source.at[:, pl.ds(128 * h, 128)],
                full.at[h, row],
                xsem.at[(1 if flow == D0 else 3) + h],
                rsem.at[flow, row],
                (row, t),
            ).start()

    @pl.when(col == 0)
    def _():
        along_row(D0, design)

    def z_send(flow, src=None):
        slot = rslot(y, zh)
        send(flow, slot, at(zh_=zh + 1), src=src)
        send(flow, slot, at(zh_=zh - 1), src=src)

    def y_send(flow, zz, src=None):
        slot = rslot(y, zz)
        send(flow, slot, at(y_=y + 1), src=src)
        send(flow, slot, at(y_=y - 1), src=src)

    def z_down(flow):
        slot = rslot(y, zh - 1)
        arrived(flow, slot)
        send(flow, slot, at(zh_=zh + 1), half=0)
        y_send(flow, zh - 1)

    def z_up(flow):
        slot = rslot(y, zh + 1)
        arrived(flow, slot)
        send(flow, slot, at(zh_=zh - 1), half=1)
        y_send(flow, zh + 1)

    def z_far(flow):
        arrived(flow, rslot(y, zh + 2))
        y_send(flow, zh + 2)

    def y_near(flow, zz):
        slot = rslot(y - 1, zz)
        arrived(flow, slot)
        send(flow, slot, at(y_=y + 1), half=0)
        slot = rslot(y + 1, zz)
        arrived(flow, slot)
        send(flow, slot, at(y_=y - 1), half=1)

    def y_far(flow, zz):
        arrived(flow, rslot(y + 2, zz))

    def flip_send(flow, src, which):
        @pl.when(off_diag)
        def _():
            other(src, bufs[flow].at[row], xsem.at[which], rsem.at[flow, row], flip).start()

    def l_send(flow):
        slot = kslot(zl, x)
        for d in (1, 2, 3):
            send(flow, slot, at(zl_=zl + d))

    def x_send(flow, ll):
        slot = kslot(ll, x)
        send(flow, slot, at(x_=x + 1))
        send(flow, slot, at(x_=x - 1))

    def x_near(flow, ll):
        slot = kslot(ll, x - 1)
        arrived(flow, slot)
        send(flow, slot, at(x_=x + 1), half=0)
        slot = kslot(ll, x + 1)
        arrived(flow, slot)
        send(flow, slot, at(x_=x - 1), half=1)

    def x_far(flow, ll):
        arrived(flow, kslot(ll, x + 2))

    def share(flow, d):
        full = dr if flow == DR else nr
        first = 4 * lax.rem(zl + d, 4)
        part = full.at[s, pl.ds(first, 4)]
        return other(part, part, psem.at[flow - DR, d, 0], psem.at[flow - DR, d, 1], partner)

    def share_wait(flow, d):
        full = dr if flow == DR else nr
        first = 4 * lax.rem(zl + d, 4)
        part = full.at[1 - s, pl.ds(first, 4)]
        other(part, part, psem.at[flow - DR, d, 0], psem.at[flow - DR, d, 1], partner).wait_recv()

    def share_corner(flow):
        full, which = (d0, 0) if flow == D0 else (n0, 1)
        return other(full.at[s], full.at[s], qsem.at[which, 0], qsem.at[which, 1], partner)

    def share_corner_wait(flow):
        full, which = (d0, 0) if flow == D0 else (n0, 1)
        other(full.at[1 - s], full.at[1 - s], qsem.at[which, 0], qsem.at[which, 1], partner).wait_recv()

    z_send(DK, design)
    y_send(DK, zh, design)
    flip_send(DR, design, 5)
    own.wait()

    @pl.when(col != 0)
    def _():
        arrived(D0, row)

    @pl.when(col == 0)
    def _():
        own_corner.wait()

    z_send(D0)
    y_send(D0, zh)
    y_near(DK, zh)

    @pl.when(row != 0)
    def _():
        arrived(NK, row)

    @pl.when(row == 0)
    def _():
        own_strip.wait()

    @pl.when(col == 0)
    def _():
        along_row(N0, nk.at[row])
        pltpu.make_async_copy(nk.at[row, :, pl.ds(0, 128)], n0.at[0, row], lsem.at[4]).start()
        pltpu.make_async_copy(nk.at[row, :, pl.ds(0, 128)], n0.at[0, row], lsem.at[4]).wait()

    z_send(NK)
    y_send(NK, zh)
    flip_send(NR, nk.at[row], 6)
    z_down(DK)
    z_up(DK)
    y_near(D0, zh)
    z_down(D0)
    z_up(D0)

    @pl.when(col != 0)
    def _():
        arrived(N0, row)

    z_send(N0)
    y_send(N0, zh)

    @pl.when(off_diag)
    def _():
        arrived(DR, k)

    @pl.when(k == row)
    def _():
        own_flip.wait()

    l_send(DR)
    x_send(DR, zl)
    y_near(DK, zh - 1)
    y_near(DK, zh + 1)
    z_far(DK)
    z_far(D0)
    y_near(D0, zh - 1)
    y_near(D0, zh + 1)
    y_near(D0, zh + 2)
    y_near(DK, zh + 2)
    y_near(NK, zh)
    x_near(DR, zl)
    z_down(NK)
    z_up(NK)
    y_near(N0, zh)
    z_down(N0)
    z_up(N0)
    for d in (1, 3, 2):
        arrived(DR, kslot(zl + d, x))
        x_send(DR, zl + d)

    @pl.when(off_diag)
    def _():
        arrived(NR, k)

    @pl.when(k == row)
    def _():
        pltpu.make_async_copy(nk.at[row], nr.at[s, k], lsem.at[5]).start()
        pltpu.make_async_copy(nk.at[row], nr.at[s, k], lsem.at[5]).wait()

    l_send(NR)
    x_send(NR, zl)
    for zz in (-1, 1):
        y_near(NK, zh + zz)
        y_near(N0, zh + zz)
    z_far(N0)
    z_far(NK)
    x_far(DR, zl)
    share(DR, 0).start()
    for d in (1, 3, 2):
        x_near(DR, zl + d)
    y_near(N0, zh + 2)
    y_near(NK, zh + 2)
    x_near(NR, zl)
    for d in (1, 3, 2):
        arrived(NR, kslot(zl + d, x))
        x_send(NR, zl + d)
    for zz in (0, -1, 1, 2):
        y_far(D0, zh + zz)
    share_corner(D0).start()
    for zz in (0, -1, 1, 2):
        y_far(N0, zh + zz)
    share_corner(N0).start()
    for d in (1, 3, 2):
        x_far(DR, zl + d)
        share(DR, d).start()
    for d in (1, 3, 2):
        x_near(NR, zl + d)
    for d in (0, 1, 3, 2):
        x_far(NR, zl + d)
        share(NR, d).start()
    for zz in (0, -1, 1, 2):
        y_far(DK, zh + zz)
        y_far(NK, zh + zz)

    share_corner_wait(D0)
    share_corner_wait(N0)
    for d in range(4):
        share_wait(DR, (4 - 0 + d) % 4)
    for d in range(4):
        share_wait(NR, d)
    share_corner(D0).wait_send()
    share_corner(N0).wait_send()
    for d in range(4):
        share(DR, d).wait_send()
        share(NR, d).wait_send()
    for flow in range(6):
        part = bufs[flow].at[pl.ds(0, 15)]
        other(part, part, ssem.at[flow], rsem.at[flow, 0], partner).wait_send()

    @pl.when(off_diag)
    def _():
        other(design, design, xsem.at[5], rsem.at[DR, 0], partner).wait_send()
        other(nk.at[0], nk.at[0], xsem.at[6], rsem.at[NR, 0], partner).wait_send()

    @pl.when(row == 0)
    def _():
        part = nk.at[pl.ds(0, 15)]
        other(part, part, xsem.at[0], rsem.at[NK, 0], partner).wait_send()

    @pl.when(col == 0)
    def _():
        for full, first in ((d0, 1), (n0, 3)):
            part = full.at[0, pl.ds(0, 15)]
            other(part, part, xsem.at[first], rsem.at[D0, 0], partner).wait_send()
            other(full.at[1], full.at[1], xsem.at[first + 1], rsem.at[D0, 0], partner).wait_send()


def gather_all(design, normals):
    f32 = jnp.float32
    wide = design.shape[1]
    shapes = [
        (16, P_SIZE, wide),
        (2, 16, P_SIZE, wide),
        (2, 16, P_SIZE, 128),
        (16, 16, wide),
        (2, 16, 16, wide),
        (2, 16, 16, 128),
    ]
    dma = pltpu.SemaphoreType.DMA
    return pl.pallas_call(
        comm_kernel,
        out_shape=[jax.ShapeDtypeStruct(shape, f32) for shape in shapes],
        in_specs=[pl.BlockSpec(memory_space=VMEM), pl.BlockSpec(memory_space=pl.ANY)],
        out_specs=[pl.BlockSpec(memory_space=VMEM)] * 6,
        scratch_shapes=[dma((6,)), dma((6, 16)), dma((7,)), dma((2, 4, 2)), dma((2, 2)), dma((6,))],
        compiler_params=pltpu.CompilerParams(collective_id=0, has_side_effects=True),
    )(design, normals)


def dot(a, b, da=1, db=0, precision=HIGHEST):
    return lax.dot_general(a, b, (((da,), (db,)), ((), ())), precision=precision, preferred_element_type=jnp.float32)


def split(a):
    high = a.astype(jnp.bfloat16)
    return high, (a - high.astype(jnp.float32)).astype(jnp.bfloat16)


def dot3(a, b, da=0, db=0):
    (ah, al), (bh, bl) = a, b
    return dot(ah, bh, da, db, None) + (dot(ah, bl, da, db, None) + dot(al, bh, da, db, None))


def iota(shape, dim):
    return lax.broadcasted_iota(jnp.int32, shape, dim)


def inverse_factor(a, w, n, nb):
    w[...] = (iota((n, n), 0) == iota((n, n), 1)).astype(jnp.float32)
    for o in range(0, n, nb):
        e = o + nb
        eye = (iota((nb, nb), 0) == iota((nb, nb), 1)).astype(jnp.float32)
        m = jnp.concatenate([a[o:e, o:e], eye], axis=1)
        below = iota((nb, 1), 0)
        for t in range(nb - 1):
            pivot = m[t : t + 1, t : t + 1]
            scaled = m[t : t + 1, :] * (1.0 / pivot)
            weight = jnp.where(below > t, m[:, t : t + 1], 0.0)
            m = m - weight * scaled
        diag = jnp.sum(m[:, :nb] * eye, axis=1, keepdims=True)
        own = m[:, nb:] * (1.0 / jnp.sqrt(diag))
        left = dot(own, w[o:e, :e])
        w[o:e, :e] = left
        if e < n:
            right = dot(own, a[o:e, e:])
            a[e:, e:] -= dot(right, right, 0, 0)
            w[e:, :e] -= dot(right, left, 0, 0)


def compute_kernel(nb, normals, dk, dr, d0, nk, nr, n0, filters, regular, out, toeplitz, fk, fr, corner, inverse):
    row = lax.axis_index("row")
    col = lax.axis_index("col")
    rows, cols = normals.shape
    step = 4 * P_SIZE
    toeplitz[...] = jnp.zeros_like(toeplitz)
    for i in range(4):
        here = slice(P_SIZE * i, P_SIZE * (i + 1))
        toeplitz[here, P_SIZE * i : P_SIZE * (i + 1)] = filters[1]
        toeplitz[here, P_SIZE * (i + 1) : P_SIZE * (i + 2)] = filters[0]
    taps = toeplitz[...]

    def filtered(data):
        parts = [dot(taps[:, P_SIZE:], data[:step, :])]
        for o in range(step, OBS, step):
            parts.append(dot(taps, data[o - P_SIZE : o + step, :]))
        return jnp.concatenate(parts, axis=0)

    f0 = filtered(jnp.concatenate([d0[0], d0[1]], axis=1))
    reg0 = jnp.where(iota((B, B), 0) == iota((B, B), 1), regular[:, :B], 0.0)
    corner[...] = jnp.concatenate([n0[0], n0[1]], axis=1) + dot(f0, f0, 0, 0) + reg0
    inverse_factor(corner, inverse, B, nb)
    w = inverse[...]
    f0s = split(f0)
    fk[...] = filtered(dk)
    fks = split(fk[...])

    def strip(base, data, first, width):
        reg = regular[:, pl.ds(pl.multiple_of(first, 128), width)]
        same = iota((B, width), 0) == iota((B, width), 1) + first
        return base + dot3(f0s, data) + jnp.where(same, reg, 0.0)

    pk = dot(w, strip(nk[...], fks, cols * col, cols))
    pks = split(pk)
    half = rows // 2
    reg = regular[:, pl.ds(pl.multiple_of(cols * col, 128), cols)]
    for h in range(2):
        fr[...] = filtered(dr.at[h])
        frs = split(fr[...])
        first = row * rows + half * h
        side = strip(nr[h], frs, first, half)
        pr = dot(w, side)
        same = iota((half, cols), 0) + first == iota((half, cols), 1) + cols * col
        here = slice(half * h, half * (h + 1))
        tile = normals[here, :] + jnp.where(same, reg, 0.0) + dot3(frs, fks)
        out[here, :] = tile - dot3(split(pr), pks)

        @pl.when(col == 0)
        def _():
            out[here, :B] = dot(side, w, 0, 1)


def local_step(nb, normals, gathered, filters, regular):
    dk, dr, d0, nk, nr, n0 = gathered
    rows, cols = normals.shape
    f32 = jnp.float32
    return pl.pallas_call(
        functools.partial(compute_kernel, nb),
        out_shape=jax.ShapeDtypeStruct((rows, cols), f32),
        in_specs=[pl.BlockSpec(memory_space=VMEM)] * 9,
        out_specs=pl.BlockSpec(memory_space=VMEM),
        scratch_shapes=[
            VMEM((4 * P_SIZE, 5 * P_SIZE), f32),
            VMEM((OBS, cols), f32),
            VMEM((OBS, cols), f32),
            VMEM((B, B), f32),
            VMEM((B, B), f32),
        ],
    )(
        normals,
        dk.reshape(OBS, cols),
        dr.reshape(2, OBS, cols),
        d0.reshape(2, OBS, 128),
        nk.reshape(B, cols),
        nr.reshape(2, B, cols),
        n0.reshape(2, B, 128),
        filters,
        regular.reshape(1, -1),
    )


def body(normals, design, filter_blocks, regular):
    gathered = gather_all(design, normals)
    return local_step(64, normals, gathered, filter_blocks, regular)


def solution(mesh):
    in_specs = (P("row", "col"), P("row", "col"), P(), P())
    out_specs = P("row", "col")
    return jax.shard_map(body, mesh=mesh, in_specs=in_specs, out_specs=out_specs, check_vma=False)
```

```python
import functools

import jax
import jax.numpy as jnp
from jax import lax
from jax.experimental import pallas as pl
from jax.experimental.pallas import tpu as pltpu
from jax.sharding import PartitionSpec as P

B = 256
P_SIZE = 32
OBS = 512
MESH = pl.DeviceIdType.MESH
VMEM = pltpu.VMEM
HIGHEST = lax.Precision.HIGHEST

DK, D0, NK, N0, DR, NR, HOP = range(7)


def comm_kernel(design, normals, dk, dr, d0, nk, nr, n0, hop, ssem, rsem, xsem, psem, lsem):
    row = lax.axis_index("row")
    col = lax.axis_index("col")
    s = lax.rem(col, 2)
    k = lax.div(col, 2)
    x, zl = lax.rem(k, 4), lax.div(k, 4)
    y, zh = lax.div(row, 4), lax.rem(row, 4)

    def at(y_=None, zh_=None, zl_=None, x_=None, s_=None):
        y_ = y if y_ is None else lax.rem(y_ + 4, 4)
        zh_ = zh if zh_ is None else lax.rem(zh_ + 4, 4)
        zl_ = zl if zl_ is None else lax.rem(zl_ + 4, 4)
        x_ = x if x_ is None else lax.rem(x_ + 4, 4)
        s_ = s if s_ is None else s_
        return (4 * y_ + zh_, 8 * zl_ + 2 * x_ + s_)

    def slot_of(a, b):
        return 4 * lax.rem(a + 4, 4) + lax.rem(b + 4, 4)

    partner = at(s_=1 - s)
    top = row == 0
    side = col == 0
    home = zl == y
    source = zh == x

    barrier = pltpu.get_barrier_semaphore()

    def hello(device):
        pl.semaphore_signal(barrier, inc=1, device_id=device, device_id_type=MESH)

    near = [at(zh_=zh + 1), at(zh_=zh - 1), partner]
    for d in (1, 2, 3):
        near += [at(y_=y + d), at(x_=x + d), at(zl_=zl + d)]
    for device in near:
        hello(device)

    @pl.when(col != 0)
    def _():
        hello((row, 0))

    def copy(src, dst, which):
        return pltpu.make_async_copy(src, dst, lsem.at[which])

    own = copy(design, dk.at[row], 0)
    own.start()
    own_hop = copy(design, hop, 1)
    own_corner = copy(design.at[:, pl.ds(0, 128)], d0.at[0, row], 2)
    own_n0 = copy(normals.at[pl.ds(0, 8), pl.ds(0, B)], n0.at[0, 0], 3)
    own_nk = [copy(normals.at[pl.ds(32 * u, 32), :], nk.at[pl.ds(32 * u, 32), :], 4 + u) for u in range(2)]
    own_nr = [copy(normals.at[pl.ds(48 * u, 48), pl.ds(0, B)], nr.at[0, 0, pl.ds(48 * u, 48)], 6 + u) for u in range(2)]
    own_dr = copy(hop, dr.at[s, slot_of(y, x)], 8)

    @pl.when(source)
    def _():
        own_hop.start()

    @pl.when(top)
    def _():
        own_nk[0].start()
        own_nk[1].start()

    @pl.when(side)
    def _():
        own_corner.start()
        own_nr[0].start()
        own_nr[1].start()

    @pl.when(top & side)
    def _():
        own_n0.start()

    one = jnp.int32(1)
    pl.semaphore_wait(barrier, len(near) + jnp.where(side, 31 * one, 0))

    def remote(src, dst, send_sem, recv_sem, device):
        return pltpu.make_async_remote_copy(
            src_ref=src, dst_ref=dst, send_sem=send_sem, recv_sem=recv_sem, device_id=device, device_id_type=MESH
        )

    def sent(part, which):
        remote(part, part, xsem.at[which], rsem.at[DK, 0], partner).wait_send()

    bufs = {DK: dk, D0: d0.at[s], DR: dr.at[s]}

    def part_of(flow, slot, half=None):
        buf = bufs[flow]
        if half is None:
            return buf.at[slot]
        return buf.at[slot, pl.ds(16 * half, 16), :]

    def send(flow, slot, device, half=None, src=None, sem=None):
        part = part_of(flow, slot, half)
        sem = ssem.at[flow] if sem is None else sem
        remote(part if src is None else src, part, sem, rsem.at[flow, slot], device).start()

    def arrived(flow, slot):
        part = part_of(flow, slot)
        remote(part, part, ssem.at[flow], rsem.at[flow, slot], partner).wait_recv()

    @pl.when(side)
    def _():
        for t in range(1, 32):
            h = t % 2
            remote(design.at[:, pl.ds(128 * h, 128)], d0.at[h, row], xsem.at[h], rsem.at[D0, row], (row, t)).start()

    def n0_part(t):
        return normals.at[pl.ds(128 * (t % 2) + 8 * (t // 2), 8), pl.ds(0, B)]

    @pl.when(top & side)
    def _():
        for t in range(1, 32):
            h, q = t % 2, t // 2
            remote(n0_part(t), n0.at[h, q], xsem.at[2 + h], rsem.at[N0, q], (0, t)).start()

    def z_send(flow, src=None):
        slot = slot_of(y, zh)
        send(flow, slot, at(zh_=zh + 1), src=src)
        send(flow, slot, at(zh_=zh - 1), src=src)

    def y_send(flow, zz, src=None):
        slot = slot_of(y, zz)
        send(flow, slot, at(y_=y + 1), src=src)
        send(flow, slot, at(y_=y - 1), src=src)
        if flow == D0:
            send(flow, slot, at(y_=y + 2))

    def spread(d):
        @pl.when(source)
        def _():
            remote(dk.at[slot_of(y, zh + d)], hop, xsem.at[4], rsem.at[HOP, 0], at(x_=x + d)).start()

    def z_near(flow, d):
        slot = slot_of(y, zh + d)
        arrived(flow, slot)
        send(flow, slot, at(zh_=zh - d), half=0 if d < 0 else 1)
        if flow == DK:
            spread(d)
        y_send(flow, zh + d)

    def z_far(flow):
        arrived(flow, slot_of(y, zh + 2))
        if flow == DK:
            spread(2)
        y_send(flow, zh + 2)

    def y_near(flow, zz):
        for d in (-1, 1):
            slot = slot_of(y + d, zz)
            arrived(flow, slot)
            send(flow, slot, at(y_=y - d), half=0 if d < 0 else 1)

    def y_far(flow, zz):
        if flow == D0:
            arrived(flow, slot_of(y - 1, zz))
            arrived(flow, slot_of(y + 1, zz))
        arrived(flow, slot_of(y + 2, zz))

    def to_home():
        @pl.when(zh != x)
        def _():
            remote(hop, hop, xsem.at[4], rsem.at[HOP, 0], partner).wait_recv()

        @pl.when(source)
        def _():
            own_hop.wait()

        slot = slot_of(y, x)

        @pl.when(home)
        def _():
            own_dr.start()

        @pl.when(zl != y)
        def _():
            remote(hop, dr.at[s, slot], xsem.at[5], rsem.at[DR, slot], at(y_=zl)).start()

    up = (zl >= y) & (zl < 3)
    down = (zl <= y) & (zl > 0)

    def along(d):
        slot = slot_of(y + d, x)
        if d == 0:

            @pl.when(home)
            def _():
                own_dr.wait()

            @pl.when(zl != y)
            def _():
                arrived(DR, slot)
        else:
            arrived(DR, slot)

        @pl.when(up)
        def _():
            send(DR, slot, at(zl_=zl + 1), sem=xsem.at[6])

        @pl.when(down)
        def _():
            send(DR, slot, at(zl_=zl - 1), sem=xsem.at[7])

        send(DR, slot, at(x_=x + 1))
        send(DR, slot, at(x_=x - 1))

    def x_near(d):
        for e in (-1, 1):
            slot = slot_of(y + d, x + e)
            arrived(DR, slot)
            send(DR, slot, at(x_=x - e), half=0 if e < 0 else 1)

    def x_far(d):
        arrived(DR, slot_of(y + d, x + 2))

    def nk_part(yy, u, half=None):
        first = 64 * lax.rem(yy + 4, 4) + 32 * u
        if half is None:
            return nk.at[pl.ds(first, 32), :]
        return nk.at[pl.ds(first + 16 * half, 16), :]

    def nk_sem(yy, u):
        return rsem.at[NK, 2 * lax.rem(yy + 4, 4) + u]

    def nk_send(yy, u, device, sem, half=None):
        part = nk_part(yy, u, half)
        remote(part, part, sem, nk_sem(yy, u), device).start()

    def nk_arrived(yy, u):
        part = nk_part(yy, u)
        remote(part, part, ssem.at[NK], nk_sem(yy, u), partner).wait_recv()

    def nk_own(u):
        @pl.when(top)
        def _():
            own_nk[u].wait()

        @pl.when(row != 0)
        def _():
            nk_arrived(y, u)

        @pl.when(zh != (3 if u == 0 else 1))
        def _():
            nk_send(y, u, at(zh_=zh + (1 if u == 0 else -1)), xsem.at[8 + u])

        nk_send(y, u, at(y_=y + 1), ssem.at[NK])
        nk_send(y, u, at(y_=y - 1), ssem.at[NK])

    def nk_near(u):
        for d in (-1, 1):
            nk_arrived(y + d, u)
            nk_send(y + d, u, at(y_=y - d), ssem.at[NK], half=0 if d < 0 else 1)

    @pl.when(top)
    def _():
        for t in (1, 3, 2):
            for u in range(2):
                src = normals.at[pl.ds(64 * t + 32 * u, 32), :]
                remote(src, nk_part(t, u), xsem.at[10], nk_sem(t, u), (4 * t, col)).start()

    def nr_part(xx, u):
        return nr.at[s, lax.rem(xx + 4, 4), pl.ds(48 * u, 48), :]

    def nr_sem(xx, u):
        return rsem.at[NR, 2 * lax.rem(xx + 4, 4) + u]

    def nr_send(xx, u, device, sem):
        part = nr_part(xx, u)
        remote(part, part, sem, nr_sem(xx, u), device).start()

    def nr_arrived(xx, u):
        part = nr_part(xx, u)
        remote(part, part, ssem.at[NR], nr_sem(xx, u), partner).wait_recv()

    def nr_own(u):
        @pl.when(side)
        def _():
            own_nr[u].wait()

        @pl.when(col != 0)
        def _():
            nr_arrived(x, u)

        @pl.when(zl < 3)
        def _():
            nr_send(x, u, at(zl_=zl + 1), xsem.at[11])

        nr_send(x, u, at(x_=x + 1), ssem.at[NR])
        nr_send(x, u, at(x_=x - 1), ssem.at[NR])

    def nr_near():
        for u in range(2):
            nr_arrived(x - 1, u)
            nr_arrived(x + 1, u)
            if u == 0:
                nr_send(x - 1, 0, at(x_=x + 1), ssem.at[NR])
            else:
                nr_send(x + 1, 1, at(x_=x - 1), ssem.at[NR])

    @pl.when(side)
    def _():
        for t in (2, 6, 1, 3, 7, 4, 5):
            h, q = t % 2, t // 2
            for u in range(2):
                src = normals.at[pl.ds(384 * h + 96 * q + 48 * u, 48), pl.ds(0, B)]
                dst = nr.at[h, q, pl.ds(48 * u, 48), :]
                remote(src, dst, xsem.at[12 + h], rsem.at[NR, 2 * q + u], (row, t)).start()

    def n0_send(q, device, sem):
        part = n0.at[s, q]
        remote(part, part, sem, rsem.at[N0, q], device).start()

    def n0_arrived(q):
        part = n0.at[s, q]
        remote(part, part, ssem.at[N0], rsem.at[N0, q], partner).wait_recv()

    def n0_own(level):
        if level == 0:

            @pl.when(top)
            def _():
                @pl.when(side)
                def _():
                    own_n0.wait()

                @pl.when(col != 0)
                def _():
                    n0_arrived(k)

                for d in (1, 3, 2):
                    n0_send(k, at(y_=y + d), xsem.at[14])
                n0_send(k, at(zh_=zh + 1), xsem.at[15])
                n0_send(k, at(zh_=zh - 1), xsem.at[15])
        elif level == 1:

            @pl.when((zh == 0) & (y != 0))
            def _():
                n0_arrived(k)
                n0_send(k, at(zh_=zh + 1), xsem.at[15])
                n0_send(k, at(zh_=zh - 1), xsem.at[15])
        elif level == 2:

            @pl.when(zh == 1)
            def _():
                n0_arrived(k)
                n0_send(k, at(zh_=zh + 1), xsem.at[16])

            @pl.when(zh == 3)
            def _():
                n0_arrived(k)
        else:

            @pl.when(zh == 2)
            def _():
                n0_arrived(k)

    def n0_plane(d):
        q = slot_of(zl + d, x)
        if d == 0:
            for e in (1, 2, 3):
                n0_send(q, at(zl_=zl + e), ssem.at[N0])
        else:
            n0_arrived(q)
        for e in (1, 3, 2):
            n0_send(q, at(x_=x + e), ssem.at[N0])

    def n0_rest(d):
        for e in (1, 2, 3):
            n0_arrived(slot_of(zl + d, x + e))

    def shared(which, h):
        if which < 4:
            part = dr.at[h, pl.ds(4 * lax.rem(y + which, 4), 4)]
        else:
            part = (d0, n0, nr)[which - 4].at[h]
        return remote(part, part, psem.at[which, 0], psem.at[which, 1], partner)

    def share(which):
        shared(which, s).start()

    far = lax.rem(x - zh + 4, 4) == 2
    off_home = lax.abs(zl - y)

    def only(condition, *steps):
        @pl.when(condition)
        def _():
            for step in steps:
                step[0](*step[1:])

    z_send(DK, design)
    y_send(DK, zh, design)
    own.wait()
    only(source, (to_home,))
    y_near(DK, zh)
    only(zh == 0, (nk_own, 0), (nk_own, 1))
    only(zl == 0, (nr_own, 0), (nr_own, 1))
    z_near(DK, -1)
    z_near(DK, 1)
    n0_own(0)

    @pl.when(col != 0)
    def _():
        arrived(D0, row)

    @pl.when(side)
    def _():
        own_corner.wait()

    z_send(D0)
    y_send(D0, zh)
    only(zl == 1, (nr_own, 0), (nr_own, 1))
    y_near(DK, zh - 1)
    y_near(DK, zh + 1)
    only((zh != x) & (lax.rem(x - zh + 4, 4) != 2), (to_home,))
    n0_own(1)
    only(zh == 1, (nk_own, 0))
    only(zh == 3, (nk_own, 1))
    only(zl == 2, (nr_own, 0), (nr_own, 1))
    z_near(D0, -1)
    z_near(D0, 1)
    z_far(DK)
    n0_own(2)
    only(zl == 3, (nr_own, 0), (nr_own, 1))
    only(far, (to_home,))
    only(zh == 2, (nk_own, 0), (nk_own, 1))
    y_near(DK, zh + 2)
    nr_near()
    z_far(D0)
    only(off_home == 0, *[(along, d) for d in (0, 1, 3, 2)])
    n0_own(3)
    n0_plane(0)
    only(zh == 3, (nk_own, 0))
    only(zh == 1, (nk_own, 1))
    only(off_home == 1, *[(along, d) for d in (0, 1, 3, 2)])
    for zz in (0, -1, 1, 2):
        y_far(D0, zh + zz)
    share(4)
    for d in (1, 3, 2):
        n0_plane(d)
    nk_near(0)
    nk_near(1)
    only(off_home == 2, *[(along, d) for d in (0, 1, 3, 2)])
    for d in (0, 1, 3, 2):
        n0_rest(d)
    share(5)
    nr_arrived(x + 2, 0)
    nr_arrived(x + 2, 1)
    share(6)
    only(off_home == 3, *[(along, d) for d in (0, 1, 3, 2)])
    for d in (0, 1, 3, 2):
        x_near(d)
    for zz in (0, -1, 1, 2):
        y_far(DK, zh + zz)
    nk_arrived(y + 2, 0)
    nk_arrived(y + 2, 1)
    for d in (0, 1, 3, 2):
        x_far(d)
        share(d)

    for which in range(7):
        shared(which, 1 - s).wait_recv()
    for which in range(7):
        shared(which, s).wait_send()

    def drained(part, flow):
        remote(part, part, ssem.at[flow], rsem.at[DK, 0], partner).wait_send()

    drained(dk.at[pl.ds(0, 15)], DK)
    drained(d0.at[0, pl.ds(0, 15)], D0)
    drained(dr.at[0, pl.ds(0, 12)], DR)
    drained(nk.at[pl.ds(0, 192), :], NK)
    drained(nr.at[0, pl.ds(0, 3)], NR)
    drained(n0.at[0, pl.ds(0, 15)], N0)

    @pl.when(side)
    def _():
        sent(d0.at[0, pl.ds(0, 15)], 0)
        sent(d0.at[1], 1)
        sent(nr.at[0, pl.ds(0, 3)], 12)
        sent(nr.at[1], 13)

    @pl.when(top & side)
    def _():
        sent(n0.at[0, pl.ds(0, 15)], 2)
        sent(n0.at[1], 3)

    @pl.when(source)
    def _():
        sent(dk.at[pl.ds(0, 3)], 4)

    @pl.when(zl != y)
    def _():
        sent(hop, 5)

    @pl.when(up)
    def _():
        sent(dk.at[pl.ds(0, 4)], 6)

    @pl.when(down)
    def _():
        sent(dk.at[pl.ds(0, 4)], 7)

    @pl.when(zh != 3)
    def _():
        sent(nk_part(0, 0), 8)

    @pl.when(zh != 1)
    def _():
        sent(nk_part(0, 0), 9)

    @pl.when(top)
    def _():
        sent(nk.at[pl.ds(0, 192), :], 10)
        sent(n0.at[0, pl.ds(0, 3)], 14)

    @pl.when(zl < 3)
    def _():
        sent(nr.at[0, 0], 11)

    @pl.when(zh == 0)
    def _():
        sent(n0.at[0, pl.ds(0, 2)], 15)

    @pl.when(zh == 1)
    def _():
        sent(n0.at[0, 0], 16)


def gather_all(design, normals):
    f32 = jnp.float32
    wide = design.shape[1]
    shapes = [
        (16, P_SIZE, wide),
        (2, 16, P_SIZE, wide),
        (2, 16, P_SIZE, 128),
        (B, wide),
        (2, 4, 96, B),
        (2, 16, 8, B),
    ]
    dma = pltpu.SemaphoreType.DMA
    return pl.pallas_call(
        comm_kernel,
        out_shape=[jax.ShapeDtypeStruct(shape, f32) for shape in shapes],
        in_specs=[pl.BlockSpec(memory_space=VMEM), pl.BlockSpec(memory_space=pl.ANY)],
        out_specs=[pl.BlockSpec(memory_space=VMEM)] * 6,
        scratch_shapes=[VMEM((P_SIZE, wide), f32), dma((6,)), dma((7, 16)), dma((17,)), dma((7, 2)), dma((9,))],
        compiler_params=pltpu.CompilerParams(collective_id=0, has_side_effects=True),
    )(design, normals)


def dot(a, b, da=1, db=0, precision=HIGHEST):
    return lax.dot_general(a, b, (((da,), (db,)), ((), ())), precision=precision, preferred_element_type=jnp.float32)


def split(a):
    high = a.astype(jnp.bfloat16)
    return high, (a - high.astype(jnp.float32)).astype(jnp.bfloat16)


def dot3(a, b, da=0, db=0):
    (ah, al), (bh, bl) = a, b
    return dot(ah, bh, da, db, None) + (dot(ah, bl, da, db, None) + dot(al, bh, da, db, None))


def iota(shape, dim):
    return lax.broadcasted_iota(jnp.int32, shape, dim)


def eliminate(block):
    nb = block.shape[0]
    wide = (8, 2 * nb)
    right = (iota((nb, nb), 0) == iota((nb, nb), 1)).astype(jnp.float32)
    rows = [jnp.concatenate([block[o : o + 8, :], right[o : o + 8, :]], axis=1) for o in range(0, nb, 8)]
    place = iota(wide, 0)
    done = []
    for g in range(nb // 8):
        t = 8 * g
        below = range(g + 1, nb // 8)
        lead = [jnp.broadcast_to(rows[g][j : j + 1, :], wide) for j in range(8)]
        pivots = {
            (j, c): jnp.broadcast_to(lead[j][:, t + c : t + c + 1], wide) for j in range(8) for c in range(j, 8)
        }
        weights = {(i, j): jnp.broadcast_to(rows[i][:, t + j : t + j + 1], wide) for i in below for j in range(8)}
        final = jnp.zeros(wide, jnp.float32)
        diag = jnp.ones(wide, jnp.float32)
        for j in range(8):
            inverse = 1.0 / pivots[j, j]
            for c in range(j + 1, 8):
                ratio = pivots[j, c] * inverse
                for d in range(c, 8):
                    pivots[c, d] = pivots[c, d] - ratio * pivots[j, d]
                lead[c] = lead[c] - ratio * lead[j]
                for i in below:
                    weights[i, c] = weights[i, c] - ratio * weights[i, j]
            scaled = lead[j] * inverse
            for i in below:
                rows[i] = rows[i] - weights[i, j] * scaled
            final = jnp.where(place == j, lead[j], final)
            diag = jnp.where(place == j, pivots[j, j], diag)
        done.append((final * (1.0 / jnp.sqrt(diag)))[:, nb:])
    return jnp.concatenate(done, axis=0)


def inverse_factor(a, w, n, nb):
    w[...] = (iota((n, n), 0) == iota((n, n), 1)).astype(jnp.float32)
    for o in range(0, n, nb):
        e = o + nb
        own = eliminate(a[o:e, o:e])
        left = dot(own, w[o:e, :e])
        w[o:e, :e] = left
        if e < n:
            right = dot(own, a[o:e, e:])
            a[e:, e:] -= dot(right, right, 0, 0)
            w[e:, :e] -= dot(right, left, 0, 0)


def compute_kernel(nb, normals, dk, dr, d0, nk, nr, n0, filters, regular, out, toeplitz, fk, fr, corner, inverse):
    row = lax.axis_index("row")
    col = lax.axis_index("col")
    rows, cols = normals.shape
    step = 4 * P_SIZE
    toeplitz[...] = jnp.zeros_like(toeplitz)
    for i in range(4):
        here = slice(P_SIZE * i, P_SIZE * (i + 1))
        toeplitz[here, P_SIZE * i : P_SIZE * (i + 1)] = filters[1]
        toeplitz[here, P_SIZE * (i + 1) : P_SIZE * (i + 2)] = filters[0]
    taps = toeplitz[...]

    def filtered(data):
        parts = [dot(taps[:, P_SIZE:], data[:step, :])]
        for o in range(step, OBS, step):
            parts.append(dot(taps, data[o - P_SIZE : o + step, :]))
        return jnp.concatenate(parts, axis=0)

    f0 = filtered(jnp.concatenate([d0[0], d0[1]], axis=1))
    reg0 = jnp.where(iota((B, B), 0) == iota((B, B), 1), regular[:, :B], 0.0)
    corner[...] = n0[...] + dot(f0, f0, 0, 0) + reg0
    inverse_factor(corner, inverse, B, nb)
    w = inverse[...]
    f0s = split(f0)
    fk[...] = filtered(dk)
    fks = split(fk[...])

    def strip(base, data, first, width):
        reg = regular[:, pl.ds(pl.multiple_of(first, 128), width)]
        same = iota((B, width), 0) == iota((B, width), 1) + first
        return base + dot3(f0s, data) + jnp.where(same, reg, 0.0)

    pk = dot(w, strip(nk[...], fks, cols * col, cols))
    pks = split(pk)
    half = rows // 2
    reg = regular[:, pl.ds(pl.multiple_of(cols * col, 128), cols)]
    for h in range(2):
        here = slice(half * h, half * (h + 1))
        first = row * rows + half * h
        fr[...] = filtered(dr.at[h])
        frs = split(fr[...])
        same = iota((half, B), 0) + first == iota((half, B), 1)
        pr = dot(nr[here, :] + dot3(frs, f0s) + jnp.where(same, regular[:, :B], 0.0), w, 1, 1)
        same = iota((half, cols), 0) + first == iota((half, cols), 1) + cols * col
        tile = normals[here, :] + jnp.where(same, reg, 0.0) + dot3(frs, fks)
        out[here, :] = tile - dot3(split(pr), pks, 1, 0)

        @pl.when(col == 0)
        def _():
            out[here, :B] = pr


def local_step(nb, normals, gathered, filters, regular):
    dk, dr, d0, nk, nr, n0 = gathered
    rows, cols = normals.shape
    f32 = jnp.float32
    return pl.pallas_call(
        functools.partial(compute_kernel, nb),
        out_shape=jax.ShapeDtypeStruct((rows, cols), f32),
        in_specs=[pl.BlockSpec(memory_space=VMEM)] * 9,
        out_specs=pl.BlockSpec(memory_space=VMEM),
        scratch_shapes=[
            VMEM((4 * P_SIZE, 5 * P_SIZE), f32),
            VMEM((OBS, cols), f32),
            VMEM((OBS, cols), f32),
            VMEM((B, B), f32),
            VMEM((B, B), f32),
        ],
    )(
        normals,
        dk.reshape(OBS, cols),
        dr.reshape(2, OBS, cols),
        d0.reshape(2, OBS, 128),
        nk,
        nr.reshape(rows, B),
        n0.reshape(B, B),
        filters,
        regular.reshape(1, -1),
    )


def body(normals, design, filter_blocks, regular):
    gathered = gather_all(design, normals)
    return local_step(128, normals, gathered, filter_blocks, regular)


def solution(mesh):
    in_specs = (P("row", "col"), P("row", "col"), P(), P())
    out_specs = P("row", "col")
    return jax.shard_map(body, mesh=mesh, in_specs=in_specs, out_specs=out_specs, check_vma=False)
```

```python
import functools

import jax
import jax.numpy as jnp
from jax import lax
from jax.experimental import pallas as pl
from jax.experimental.pallas import tpu as pltpu
from jax.sharding import PartitionSpec as P

B = 256
P_SIZE = 32
OBS = 512
MESH = pl.DeviceIdType.MESH
VMEM = pltpu.VMEM
HIGHEST = lax.Precision.HIGHEST

DK, D0, NK, N0, DR, NR, HOP = range(7)


def kernel(design, normals, filters, regular, out, *scratch):
    (dk, dr, d0, nk, nr, n0, hop, ssem, rsem, xsem, psem, lsem) = scratch[:12]
    (tile, result, toeplitz, f0, fk, fr, corner, inverse) = scratch[12:]
    row = lax.axis_index("row")
    col = lax.axis_index("col")
    s = lax.rem(col, 2)
    k = lax.div(col, 2)
    x, zl = lax.rem(k, 4), lax.div(k, 4)
    y, zh = lax.div(row, 4), lax.rem(row, 4)

    def at(y_=None, zh_=None, zl_=None, x_=None, s_=None):
        y_ = y if y_ is None else lax.rem(y_ + 4, 4)
        zh_ = zh if zh_ is None else lax.rem(zh_ + 4, 4)
        zl_ = zl if zl_ is None else lax.rem(zl_ + 4, 4)
        x_ = x if x_ is None else lax.rem(x_ + 4, 4)
        s_ = s if s_ is None else s_
        return (4 * y_ + zh_, 8 * zl_ + 2 * x_ + s_)

    def slot_of(a, b):
        return 4 * lax.rem(a + 4, 4) + lax.rem(b + 4, 4)

    partner = at(s_=1 - s)
    top = row == 0
    side = col == 0
    home = zl == y
    source = zh == x

    barrier = pltpu.get_barrier_semaphore()

    def hello(device):
        pl.semaphore_signal(barrier, inc=1, device_id=device, device_id_type=MESH)

    near = [at(zh_=zh + 1), at(zh_=zh - 1), partner]
    for d in (1, 2, 3):
        near += [at(y_=y + d), at(x_=x + d), at(zl_=zl + d)]
    for device in near:
        hello(device)

    @pl.when(col != 0)
    def _():
        hello((row, 0))

    def copy(src, dst, which):
        return pltpu.make_async_copy(src, dst, lsem.at[which])

    own = copy(design, dk.at[row], 0)
    own.start()
    own_tile = copy(normals, tile, 9)
    own_tile.start()
    own_hop = copy(design, hop, 1)
    own_corner = copy(design.at[:, pl.ds(0, 128)], d0.at[0, row], 2)
    own_n0 = copy(normals.at[pl.ds(0, 8), pl.ds(0, B)], n0.at[0, 0], 3)
    own_nk = [copy(normals.at[pl.ds(32 * u, 32), :], nk.at[pl.ds(32 * u, 32), :], 4 + u) for u in range(2)]
    own_nr = [copy(normals.at[pl.ds(48 * u, 48), pl.ds(0, B)], nr.at[0, 0, pl.ds(48 * u, 48)], 6 + u) for u in range(2)]
    own_dr = copy(hop, dr.at[s, slot_of(y, x)], 8)

    @pl.when(source)
    def _():
        own_hop.start()

    @pl.when(top)
    def _():
        own_nk[0].start()
        own_nk[1].start()

    @pl.when(side)
    def _():
        own_corner.start()
        own_nr[0].start()
        own_nr[1].start()

    @pl.when(top & side)
    def _():
        own_n0.start()

    one = jnp.int32(1)
    pl.semaphore_wait(barrier, len(near) + jnp.where(side, 31 * one, 0))

    def remote(src, dst, send_sem, recv_sem, device):
        return pltpu.make_async_remote_copy(
            src_ref=src, dst_ref=dst, send_sem=send_sem, recv_sem=recv_sem, device_id=device, device_id_type=MESH
        )

    def sent(part, which):
        remote(part, part, xsem.at[which], rsem.at[DK, 0], partner).wait_send()

    bufs = {DK: dk, D0: d0.at[s], DR: dr.at[s]}

    def part_of(flow, slot, half=None):
        buf = bufs[flow]
        if half is None:
            return buf.at[slot]
        return buf.at[slot, pl.ds(16 * half, 16), :]

    def send(flow, slot, device, half=None, src=None, sem=None):
        part = part_of(flow, slot, half)
        sem = ssem.at[flow] if sem is None else sem
        remote(part if src is None else src, part, sem, rsem.at[flow, slot], device).start()

    def arrived(flow, slot):
        part = part_of(flow, slot)
        remote(part, part, ssem.at[flow], rsem.at[flow, slot], partner).wait_recv()

    @pl.when(side)
    def _():
        for t in range(1, 32):
            h = t % 2
            remote(design.at[:, pl.ds(128 * h, 128)], d0.at[h, row], xsem.at[h], rsem.at[D0, row], (row, t)).start()

    def n0_part(t):
        return normals.at[pl.ds(128 * (t % 2) + 8 * (t // 2), 8), pl.ds(0, B)]

    @pl.when(top & side)
    def _():
        for t in range(1, 32):
            h, q = t % 2, t // 2
            remote(n0_part(t), n0.at[h, q], xsem.at[2 + h], rsem.at[N0, q], (0, t)).start()

    def z_send(flow, src=None):
        slot = slot_of(y, zh)
        send(flow, slot, at(zh_=zh + 1), src=src)
        send(flow, slot, at(zh_=zh - 1), src=src)

    def y_send(flow, zz, src=None):
        slot = slot_of(y, zz)
        send(flow, slot, at(y_=y + 1), src=src)
        send(flow, slot, at(y_=y - 1), src=src)
        if flow == D0:
            send(flow, slot, at(y_=y + 2))

    def spread(d):
        @pl.when(source)
        def _():
            remote(dk.at[slot_of(y, zh + d)], hop, xsem.at[4], rsem.at[HOP, 0], at(x_=x + d)).start()

    def z_near(flow, d):
        slot = slot_of(y, zh + d)
        arrived(flow, slot)
        send(flow, slot, at(zh_=zh - d), half=0 if d < 0 else 1)
        if flow == DK:
            spread(d)
        y_send(flow, zh + d)

    def z_far(flow):
        arrived(flow, slot_of(y, zh + 2))
        if flow == DK:
            spread(2)
        y_send(flow, zh + 2)

    def y_near(flow, zz):
        for d in (-1, 1):
            slot = slot_of(y + d, zz)
            arrived(flow, slot)
            send(flow, slot, at(y_=y - d), half=0 if d < 0 else 1)

    def y_far(flow, zz):
        if flow == D0:
            arrived(flow, slot_of(y - 1, zz))
            arrived(flow, slot_of(y + 1, zz))
        arrived(flow, slot_of(y + 2, zz))

    def to_home():
        @pl.when(zh != x)
        def _():
            remote(hop, hop, xsem.at[4], rsem.at[HOP, 0], partner).wait_recv()

        @pl.when(source)
        def _():
            own_hop.wait()

        slot = slot_of(y, x)

        @pl.when(home)
        def _():
            own_dr.start()

        @pl.when(zl != y)
        def _():
            remote(hop, dr.at[s, slot], xsem.at[5], rsem.at[DR, slot], at(y_=zl)).start()

    up = (zl >= y) & (zl < 3)
    down = (zl <= y) & (zl > 0)

    def along(d):
        slot = slot_of(y + d, x)
        if d == 0:

            @pl.when(home)
            def _():
                own_dr.wait()

            @pl.when(zl != y)
            def _():
                arrived(DR, slot)
        else:
            arrived(DR, slot)

        @pl.when(up)
        def _():
            send(DR, slot, at(zl_=zl + 1), sem=xsem.at[6])

        @pl.when(down)
        def _():
            send(DR, slot, at(zl_=zl - 1), sem=xsem.at[7])

        send(DR, slot, at(x_=x + 1))
        send(DR, slot, at(x_=x - 1))

    def x_near(d):
        for e in (-1, 1):
            slot = slot_of(y + d, x + e)
            arrived(DR, slot)
            send(DR, slot, at(x_=x - e), half=0 if e < 0 else 1)

    def x_far(d):
        arrived(DR, slot_of(y + d, x + 2))

    def nk_part(yy, u, half=None):
        first = 64 * lax.rem(yy + 4, 4) + 32 * u
        if half is None:
            return nk.at[pl.ds(first, 32), :]
        return nk.at[pl.ds(first + 16 * half, 16), :]

    def nk_sem(yy, u):
        return rsem.at[NK, 2 * lax.rem(yy + 4, 4) + u]

    def nk_send(yy, u, device, sem, half=None):
        part = nk_part(yy, u, half)
        remote(part, part, sem, nk_sem(yy, u), device).start()

    def nk_arrived(yy, u):
        part = nk_part(yy, u)
        remote(part, part, ssem.at[NK], nk_sem(yy, u), partner).wait_recv()

    def nk_own(u):
        @pl.when(top)
        def _():
            own_nk[u].wait()

        @pl.when(row != 0)
        def _():
            nk_arrived(y, u)

        @pl.when(zh != (3 if u == 0 else 1))
        def _():
            nk_send(y, u, at(zh_=zh + (1 if u == 0 else -1)), xsem.at[8 + u])

        nk_send(y, u, at(y_=y + 1), ssem.at[NK])
        nk_send(y, u, at(y_=y - 1), ssem.at[NK])

    def nk_near(u):
        for d in (-1, 1):
            nk_arrived(y + d, u)
            nk_send(y + d, u, at(y_=y - d), ssem.at[NK], half=0 if d < 0 else 1)

    @pl.when(top)
    def _():
        for t in (1, 3, 2):
            for u in range(2):
                src = normals.at[pl.ds(64 * t + 32 * u, 32), :]
                remote(src, nk_part(t, u), xsem.at[10], nk_sem(t, u), (4 * t, col)).start()

    def nr_part(xx, u):
        return nr.at[s, lax.rem(xx + 4, 4), pl.ds(48 * u, 48), :]

    def nr_sem(xx, u):
        return rsem.at[NR, 2 * lax.rem(xx + 4, 4) + u]

    def nr_send(xx, u, device, sem):
        part = nr_part(xx, u)
        remote(part, part, sem, nr_sem(xx, u), device).start()

    def nr_arrived(xx, u):
        part = nr_part(xx, u)
        remote(part, part, ssem.at[NR], nr_sem(xx, u), partner).wait_recv()

    def nr_own(u):
        @pl.when(side)
        def _():
            own_nr[u].wait()

        @pl.when(col != 0)
        def _():
            nr_arrived(x, u)

        @pl.when(zl < 3)
        def _():
            nr_send(x, u, at(zl_=zl + 1), xsem.at[11])

        nr_send(x, u, at(x_=x + 1), ssem.at[NR])
        nr_send(x, u, at(x_=x - 1), ssem.at[NR])

    def nr_near():
        for u in range(2):
            nr_arrived(x - 1, u)
            nr_arrived(x + 1, u)
            if u == 0:
                nr_send(x - 1, 0, at(x_=x + 1), ssem.at[NR])
            else:
                nr_send(x + 1, 1, at(x_=x - 1), ssem.at[NR])

    @pl.when(side)
    def _():
        for t in (2, 6, 1, 3, 7, 4, 5):
            h, q = t % 2, t // 2
            for u in range(2):
                src = normals.at[pl.ds(384 * h + 96 * q + 48 * u, 48), pl.ds(0, B)]
                dst = nr.at[h, q, pl.ds(48 * u, 48), :]
                remote(src, dst, xsem.at[12 + h], rsem.at[NR, 2 * q + u], (row, t)).start()

    def n0_send(q, device, sem):
        part = n0.at[s, q]
        remote(part, part, sem, rsem.at[N0, q], device).start()

    def n0_arrived(q):
        part = n0.at[s, q]
        remote(part, part, ssem.at[N0], rsem.at[N0, q], partner).wait_recv()

    def n0_own(level):
        if level == 0:

            @pl.when(top)
            def _():
                @pl.when(side)
                def _():
                    own_n0.wait()

                @pl.when(col != 0)
                def _():
                    n0_arrived(k)

                for d in (1, 3, 2):
                    n0_send(k, at(y_=y + d), xsem.at[14])
                n0_send(k, at(zh_=zh + 1), xsem.at[15])
                n0_send(k, at(zh_=zh - 1), xsem.at[15])
        elif level == 1:

            @pl.when((zh == 0) & (y != 0))
            def _():
                n0_arrived(k)
                n0_send(k, at(zh_=zh + 1), xsem.at[15])
                n0_send(k, at(zh_=zh - 1), xsem.at[15])
        elif level == 2:

            @pl.when(zh == 1)
            def _():
                n0_arrived(k)
                n0_send(k, at(zh_=zh + 1), xsem.at[16])

            @pl.when(zh == 3)
            def _():
                n0_arrived(k)
        else:

            @pl.when(zh == 2)
            def _():
                n0_arrived(k)

    def n0_plane(d):
        q = slot_of(zl + d, x)
        if d == 0:
            for e in (1, 2, 3):
                n0_send(q, at(zl_=zl + e), ssem.at[N0])
        else:
            n0_arrived(q)
        for e in (1, 3, 2):
            n0_send(q, at(x_=x + e), ssem.at[N0])

    def n0_rest(d):
        for e in (1, 2, 3):
            n0_arrived(slot_of(zl + d, x + e))

    def shared(which, h):
        if which < 4:
            part = dr.at[h, pl.ds(4 * lax.rem(y + which, 4), 4)]
        else:
            part = (d0, n0, nr)[which - 4].at[h]
        return remote(part, part, psem.at[which, 0], psem.at[which, 1], partner)

    def share(which):
        shared(which, s).start()

    far = lax.rem(x - zh + 4, 4) == 2
    off_home = lax.abs(zl - y)

    def only(condition, *steps):
        @pl.when(condition)
        def _():
            for step in steps:
                step[0](*step[1:])

    z_send(DK, design)
    y_send(DK, zh, design)
    own.wait()
    only(source, (to_home,))
    y_near(DK, zh)
    only(zh == 0, (nk_own, 0), (nk_own, 1))
    only(zl == 0, (nr_own, 0), (nr_own, 1))
    z_near(DK, -1)
    z_near(DK, 1)
    n0_own(0)

    @pl.when(col != 0)
    def _():
        arrived(D0, row)

    @pl.when(side)
    def _():
        own_corner.wait()

    z_send(D0)
    y_send(D0, zh)
    only(zl == 1, (nr_own, 0), (nr_own, 1))
    y_near(DK, zh - 1)
    y_near(DK, zh + 1)
    only((zh != x) & (lax.rem(x - zh + 4, 4) != 2), (to_home,))
    n0_own(1)
    only(zh == 1, (nk_own, 0))
    only(zh == 3, (nk_own, 1))
    only(zl == 2, (nr_own, 0), (nr_own, 1))
    z_near(D0, -1)
    z_near(D0, 1)
    z_far(DK)
    n0_own(2)
    only(zl == 3, (nr_own, 0), (nr_own, 1))
    only(far, (to_home,))
    only(zh == 2, (nk_own, 0), (nk_own, 1))
    y_near(DK, zh + 2)
    nr_near()
    z_far(D0)
    only(off_home == 0, *[(along, d) for d in (0, 1, 3, 2)])
    n0_own(3)
    n0_plane(0)
    only(zh == 3, (nk_own, 0))
    only(zh == 1, (nk_own, 1))
    for zz in (0, -1, 1, 2):
        y_far(D0, zh + zz)
    share(4)
    only(off_home == 1, *[(along, d) for d in (0, 1, 3, 2)])
    for d in (1, 3, 2):
        n0_plane(d)
    for d in (0, 1, 3, 2):
        n0_rest(d)
    share(5)
    nk_near(0)
    nk_near(1)
    shared(4, 1 - s).wait_recv()

    def nr_far():
        nr_arrived(x + 2, 0)
        nr_arrived(x + 2, 1)
        share(6)

    def nk_far():
        nk_arrived(y + 2, 0)
        nk_arrived(y + 2, 1)

    def x_last(d):
        x_far(d)
        share(d)

    steps = [(lambda: only(off_home == 2, *[(along, d) for d in (0, 1, 3, 2)]))]
    steps += [nr_far, (lambda: only(off_home == 3, *[(along, d) for d in (0, 1, 3, 2)]))]
    steps += [functools.partial(x_near, d) for d in (0, 1, 3, 2)]
    steps += [functools.partial(y_far, DK, zh + zz) for zz in (0, -1, 1, 2)]
    steps += [nk_far] + [functools.partial(x_last, d) for d in (0, 1, 3, 2)]
    turn = [0]

    def tick():
        turn[0] += 1
        if turn[0] % 2 == 0 and steps:
            steps.pop(0)()

    rows, cols = tile.shape
    half = rows // 2
    toeplitz[...] = jnp.zeros_like(toeplitz)
    for i in range(4):
        here = slice(P_SIZE * i, P_SIZE * (i + 1))
        toeplitz[here, P_SIZE * i : P_SIZE * (i + 1)] = filters[1]
        toeplitz[here, P_SIZE * (i + 1) : P_SIZE * (i + 2)] = filters[0]

    def filtered(load, dst):
        width = dst.shape[1]
        for q in range(0, 16, 4):
            first = max(q - 1, 0)
            data = load(first, q + 4).reshape(P_SIZE * (q + 4 - first), width)
            taps = toeplitz[:, P_SIZE:] if q == 0 else toeplitz[...]
            dst[P_SIZE * q : P_SIZE * (q + 4), :] = dot(taps, data)

    filtered(lambda a, b: jnp.concatenate([d0[0, a:b], d0[1, a:b]], axis=2), f0)
    gram = dot(f0[...], f0[...], 0, 0)
    steps.pop(0)()
    shared(5, 1 - s).wait_recv()
    reg0 = jnp.where(iota((B, B), 0) == iota((B, B), 1), regular[:, :B], 0.0)
    corner[...] = n0[...].reshape(B, B) + gram + reg0
    inverse_factor(corner, inverse, B, 128, tick)
    while steps:
        steps.pop(0)()
    w = inverse[...]
    f0s = split(f0[...])
    filtered(lambda a, b: dk[a:b], fk)
    fks = split(fk[...])
    reg = regular[:, pl.ds(pl.multiple_of(cols * col, 128), cols)]
    same = iota((B, cols), 0) == iota((B, cols), 1) + cols * col
    pks = split(dot(w, nk[...] + dot3(f0s, fks) + jnp.where(same, reg, 0.0)))
    own_tile.wait()
    shared(6, 1 - s).wait_recv()
    flush = []
    for e in range(2):
        h = s if e == 0 else 1 - s
        if e == 1:
            for which in range(4):
                shared(which, h).wait_recv()
        filtered(lambda a, b: dr[h, a:b], fr)
        frs = split(fr[...])
        first = row * rows + half * h
        same = iota((half, B), 0) + first == iota((half, B), 1)
        strip = nr[h].reshape(half, B) + dot3(frs, f0s) + jnp.where(same, regular[:, :B], 0.0)
        pr = dot(strip, w, 1, 1)
        here = pl.ds(pl.multiple_of(half * h, 8), half)
        same = iota((half, cols), 0) + first == iota((half, cols), 1) + cols * col
        value = tile[here, :] + jnp.where(same, reg, 0.0) + dot3(frs, fks)
        result[e] = value - dot3(split(pr), pks, 1, 0)

        @pl.when(side)
        def _():
            result[e, :, :B] = pr

        flush.append(copy(result.at[e], out.at[here, :], 10 + e))
        flush[e].start()

    for which in range(7):
        shared(which, s).wait_send()

    def drained(part, flow):
        remote(part, part, ssem.at[flow], rsem.at[DK, 0], partner).wait_send()

    drained(dk.at[pl.ds(0, 15)], DK)
    drained(d0.at[0, pl.ds(0, 15)], D0)
    drained(dr.at[0, pl.ds(0, 12)], DR)
    drained(nk.at[pl.ds(0, 192), :], NK)
    drained(nr.at[0, pl.ds(0, 3)], NR)
    drained(n0.at[0, pl.ds(0, 15)], N0)

    @pl.when(side)
    def _():
        sent(d0.at[0, pl.ds(0, 15)], 0)
        sent(d0.at[1], 1)
        sent(nr.at[0, pl.ds(0, 3)], 12)
        sent(nr.at[1], 13)

    @pl.when(top & side)
    def _():
        sent(n0.at[0, pl.ds(0, 15)], 2)
        sent(n0.at[1], 3)

    @pl.when(source)
    def _():
        sent(dk.at[pl.ds(0, 3)], 4)

    @pl.when(zl != y)
    def _():
        sent(hop, 5)

    @pl.when(up)
    def _():
        sent(dk.at[pl.ds(0, 4)], 6)

    @pl.when(down)
    def _():
        sent(dk.at[pl.ds(0, 4)], 7)

    @pl.when(zh != 3)
    def _():
        sent(nk_part(0, 0), 8)

    @pl.when(zh != 1)
    def _():
        sent(nk_part(0, 0), 9)

    @pl.when(top)
    def _():
        sent(nk.at[pl.ds(0, 192), :], 10)
        sent(n0.at[0, pl.ds(0, 3)], 14)

    @pl.when(zl < 3)
    def _():
        sent(nr.at[0, 0], 11)

    @pl.when(zh == 0)
    def _():
        sent(n0.at[0, pl.ds(0, 2)], 15)

    @pl.when(zh == 1)
    def _():
        sent(n0.at[0, 0], 16)

    flush[0].wait()
    flush[1].wait()


def local_step(normals, design, filters, regular):
    f32 = jnp.float32
    rows, cols = normals.shape
    dma = pltpu.SemaphoreType.DMA
    blocks = [(16, P_SIZE, cols), (2, 16, P_SIZE, cols), (2, 16, P_SIZE, 128), (B, cols), (2, 4, 96, B), (2, 16, 8, B)]
    blocks += [(P_SIZE, cols)]
    sems = [dma((6,)), dma((7, 16)), dma((17,)), dma((7, 2)), dma((12,))]
    work = [(rows, cols), (2, rows // 2, cols), (4 * P_SIZE, 5 * P_SIZE), (OBS, B), (OBS, cols), (OBS, cols), (B, B), (B, B)]
    return pl.pallas_call(
        kernel,
        out_shape=jax.ShapeDtypeStruct((rows, cols), f32),
        in_specs=[pl.BlockSpec(memory_space=space) for space in (VMEM, pl.ANY, VMEM, VMEM)],
        out_specs=pl.BlockSpec(memory_space=pl.ANY),
        scratch_shapes=[VMEM(shape, f32) for shape in blocks] + sems + [VMEM(shape, f32) for shape in work],
        compiler_params=pltpu.CompilerParams(collective_id=0, has_side_effects=True),
    )(design, normals, filters, regular.reshape(1, -1))


def dot(a, b, da=1, db=0, precision=HIGHEST):
    return lax.dot_general(a, b, (((da,), (db,)), ((), ())), precision=precision, preferred_element_type=jnp.float32)


def split(a):
    high = a.astype(jnp.bfloat16)
    return high, (a - high.astype(jnp.float32)).astype(jnp.bfloat16)


def dot3(a, b, da=0, db=0):
    (ah, al), (bh, bl) = a, b
    return dot(ah, bh, da, db, None) + (dot(ah, bl, da, db, None) + dot(al, bh, da, db, None))


def iota(shape, dim):
    return lax.broadcasted_iota(jnp.int32, shape, dim)


def eliminate(block, tick):
    nb = block.shape[0]
    wide = (8, 2 * nb)
    right = (iota((nb, nb), 0) == iota((nb, nb), 1)).astype(jnp.float32)
    rows = [jnp.concatenate([block[o : o + 8, :], right[o : o + 8, :]], axis=1) for o in range(0, nb, 8)]
    place = iota(wide, 0)
    done = []
    for g in range(nb // 8):
        t = 8 * g
        below = range(g + 1, nb // 8)
        lead = [jnp.broadcast_to(rows[g][j : j + 1, :], wide) for j in range(8)]
        pivots = {
            (j, c): jnp.broadcast_to(lead[j][:, t + c : t + c + 1], wide) for j in range(8) for c in range(j, 8)
        }
        weights = {(i, j): jnp.broadcast_to(rows[i][:, t + j : t + j + 1], wide) for i in below for j in range(8)}
        final = jnp.zeros(wide, jnp.float32)
        diag = jnp.ones(wide, jnp.float32)
        for j in range(8):
            inverse = 1.0 / pivots[j, j]
            for c in range(j + 1, 8):
                ratio = pivots[j, c] * inverse
                for d in range(c, 8):
                    pivots[c, d] = pivots[c, d] - ratio * pivots[j, d]
                lead[c] = lead[c] - ratio * lead[j]
                for i in below:
                    weights[i, c] = weights[i, c] - ratio * weights[i, j]
            scaled = lead[j] * inverse
            for i in below:
                rows[i] = rows[i] - weights[i, j] * scaled
            final = jnp.where(place == j, lead[j], final)
            diag = jnp.where(place == j, pivots[j, j], diag)
        done.append((final * (1.0 / jnp.sqrt(diag)))[:, nb:])
        tick()
    return jnp.concatenate(done, axis=0)


def inverse_factor(a, w, n, nb, tick):
    w[...] = (iota((n, n), 0) == iota((n, n), 1)).astype(jnp.float32)
    for o in range(0, n, nb):
        e = o + nb
        own = eliminate(a[o:e, o:e], tick)
        left = dot(own, w[o:e, :e])
        w[o:e, :e] = left
        if e < n:
            right = dot(own, a[o:e, e:])
            a[e:, e:] -= dot(right, right, 0, 0)
            w[e:, :e] -= dot(right, left, 0, 0)


def body(normals, design, filter_blocks, regular):
    return local_step(normals, design, filter_blocks, regular)


def solution(mesh):
    in_specs = (P("row", "col"), P("row", "col"), P(), P())
    out_specs = P("row", "col")
    return jax.shard_map(body, mesh=mesh, in_specs=in_specs, out_specs=out_specs, check_vma=False)
```

```python
import functools

import jax
import jax.numpy as jnp
from jax import lax
from jax.experimental import pallas as pl
from jax.experimental.pallas import tpu as pltpu
from jax.sharding import PartitionSpec as P

B = 256
P_SIZE = 32
OBS = 512
MESH = pl.DeviceIdType.MESH
VMEM = pltpu.VMEM
HIGHEST = lax.Precision.HIGHEST

DK, D0, NK, N0, DR, NR, HOP = range(7)


def kernel(design, normals, filters, regular, out, *scratch):
    (dk, dr, d0, nk, nr, n0, hop, ssem, rsem, xsem, psem, lsem) = scratch[:12]
    (tile, result, toeplitz, f0, fk, fr, corner, inverse) = scratch[12:]
    row = lax.axis_index("row")
    col = lax.axis_index("col")
    s = lax.rem(col, 2)
    k = lax.div(col, 2)
    x, zl = lax.rem(k, 4), lax.div(k, 4)
    y, zh = lax.div(row, 4), lax.rem(row, 4)

    def at(y_=None, zh_=None, zl_=None, x_=None, s_=None):
        y_ = y if y_ is None else lax.rem(y_ + 4, 4)
        zh_ = zh if zh_ is None else lax.rem(zh_ + 4, 4)
        zl_ = zl if zl_ is None else lax.rem(zl_ + 4, 4)
        x_ = x if x_ is None else lax.rem(x_ + 4, 4)
        s_ = s if s_ is None else s_
        return (4 * y_ + zh_, 8 * zl_ + 2 * x_ + s_)

    def slot_of(a, b):
        return 4 * lax.rem(a + 4, 4) + lax.rem(b + 4, 4)

    partner = at(s_=1 - s)
    top = row == 0
    side = col == 0
    home = zl == y
    source = zh == x

    barrier = pltpu.get_barrier_semaphore()

    def hello(device):
        pl.semaphore_signal(barrier, inc=1, device_id=device, device_id_type=MESH)

    near = [at(zh_=zh + 1), at(zh_=zh - 1), partner]
    for d in (1, 2, 3):
        near += [at(y_=y + d), at(x_=x + d), at(zl_=zl + d)]
    for device in near:
        hello(device)

    @pl.when(col != 0)
    def _():
        hello((row, 0))

    def copy(src, dst, which):
        return pltpu.make_async_copy(src, dst, lsem.at[which])

    own = copy(design, dk.at[row], 0)
    own.start()
    own_tile = copy(normals, tile, 9)
    own_tile.start()
    own_hop = copy(design, hop, 1)
    own_corner = copy(design.at[:, pl.ds(0, 128)], d0.at[0, row], 2)
    own_n0 = copy(normals.at[pl.ds(0, 8), pl.ds(0, B)], n0.at[0, 0], 3)
    own_nk = [copy(normals.at[pl.ds(32 * u, 32), :], nk.at[pl.ds(32 * u, 32), :], 4 + u) for u in range(2)]
    own_nr = [copy(normals.at[pl.ds(48 * u, 48), pl.ds(0, B)], nr.at[0, 0, pl.ds(48 * u, 48)], 6 + u) for u in range(2)]
    own_dr = copy(hop, dr.at[s, slot_of(y, x)], 8)

    @pl.when(source)
    def _():
        own_hop.start()

    @pl.when(top)
    def _():
        own_nk[0].start()
        own_nk[1].start()

    @pl.when(side)
    def _():
        own_corner.start()
        own_nr[0].start()
        own_nr[1].start()

    @pl.when(top & side)
    def _():
        own_n0.start()

    one = jnp.int32(1)
    pl.semaphore_wait(barrier, len(near) + jnp.where(side, 31 * one, 0))

    def remote(src, dst, send_sem, recv_sem, device):
        return pltpu.make_async_remote_copy(
            src_ref=src, dst_ref=dst, send_sem=send_sem, recv_sem=recv_sem, device_id=device, device_id_type=MESH
        )

    def sent(part, which):
        remote(part, part, xsem.at[which], rsem.at[DK, 0], partner).wait_send()

    bufs = {DK: dk, D0: d0.at[s], DR: dr.at[s]}

    def part_of(flow, slot, half=None):
        buf = bufs[flow]
        if half is None:
            return buf.at[slot]
        return buf.at[slot, pl.ds(16 * half, 16), :]

    def send(flow, slot, device, half=None, src=None, sem=None):
        part = part_of(flow, slot, half)
        sem = ssem.at[flow] if sem is None else sem
        remote(part if src is None else src, part, sem, rsem.at[flow, slot], device).start()

    def arrived(flow, slot):
        part = part_of(flow, slot)
        remote(part, part, ssem.at[flow], rsem.at[flow, slot], partner).wait_recv()

    @pl.when(side)
    def _():
        for t in range(1, 32):
            h = t % 2
            remote(design.at[:, pl.ds(128 * h, 128)], d0.at[h, row], xsem.at[h], rsem.at[D0, row], (row, t)).start()

    def n0_part(t):
        return normals.at[pl.ds(128 * (t % 2) + 8 * (t // 2), 8), pl.ds(0, B)]

    @pl.when(top & side)
    def _():
        for t in range(1, 32):
            h, q = t % 2, t // 2
            remote(n0_part(t), n0.at[h, q], xsem.at[2 + h], rsem.at[N0, q], (0, t)).start()

    def z_send(flow, src=None):
        slot = slot_of(y, zh)
        send(flow, slot, at(zh_=zh + 1), src=src)
        send(flow, slot, at(zh_=zh - 1), src=src)

    def y_send(flow, zz, src=None):
        slot = slot_of(y, zz)
        send(flow, slot, at(y_=y + 1), src=src)
        send(flow, slot, at(y_=y - 1), src=src)
        if flow == D0:
            send(flow, slot, at(y_=y + 2))

    def spread(d):
        @pl.when(source)
        def _():
            remote(dk.at[slot_of(y, zh + d)], hop, xsem.at[4], rsem.at[HOP, 0], at(x_=x + d)).start()

    def z_near(flow, d):
        slot = slot_of(y, zh + d)
        arrived(flow, slot)
        send(flow, slot, at(zh_=zh - d), half=0 if d < 0 else 1)
        if flow == DK:
            spread(d)
        y_send(flow, zh + d)

    def z_far(flow):
        arrived(flow, slot_of(y, zh + 2))
        if flow == DK:
            spread(2)
        y_send(flow, zh + 2)

    def y_near(flow, zz):
        for d in (-1, 1):
            slot = slot_of(y + d, zz)
            arrived(flow, slot)
            send(flow, slot, at(y_=y - d), half=0 if d < 0 else 1)

    def y_far(flow, zz):
        if flow == D0:
            arrived(flow, slot_of(y - 1, zz))
            arrived(flow, slot_of(y + 1, zz))
        arrived(flow, slot_of(y + 2, zz))

    def to_home():
        @pl.when(zh != x)
        def _():
            remote(hop, hop, xsem.at[4], rsem.at[HOP, 0], partner).wait_recv()

        @pl.when(source)
        def _():
            own_hop.wait()

        slot = slot_of(y, x)

        @pl.when(home)
        def _():
            own_dr.start()

        @pl.when(zl != y)
        def _():
            remote(hop, dr.at[s, slot], xsem.at[5], rsem.at[DR, slot], at(y_=zl)).start()

    up = (zl >= y) & (zl < 3)
    down = (zl <= y) & (zl > 0)

    def along(d):
        slot = slot_of(y + d, x)
        if d == 0:

            @pl.when(home)
            def _():
                own_dr.wait()

            @pl.when(zl != y)
            def _():
                arrived(DR, slot)
        else:
            arrived(DR, slot)

        @pl.when(up)
        def _():
            send(DR, slot, at(zl_=zl + 1), sem=xsem.at[6])

        @pl.when(down)
        def _():
            send(DR, slot, at(zl_=zl - 1), sem=xsem.at[7])

        send(DR, slot, at(x_=x + 1))
        send(DR, slot, at(x_=x - 1))

    def x_near(d):
        for e in (-1, 1):
            slot = slot_of(y + d, x + e)
            arrived(DR, slot)
            send(DR, slot, at(x_=x - e), half=0 if e < 0 else 1)

    def x_far(d):
        arrived(DR, slot_of(y + d, x + 2))

    def nk_part(yy, u, half=None):
        first = 64 * lax.rem(yy + 4, 4) + 32 * u
        if half is None:
            return nk.at[pl.ds(first, 32), :]
        return nk.at[pl.ds(first + 16 * half, 16), :]

    def nk_sem(yy, u):
        return rsem.at[NK, 2 * lax.rem(yy + 4, 4) + u]

    def nk_send(yy, u, device, sem, half=None):
        part = nk_part(yy, u, half)
        remote(part, part, sem, nk_sem(yy, u), device).start()

    def nk_arrived(yy, u):
        part = nk_part(yy, u)
        remote(part, part, ssem.at[NK], nk_sem(yy, u), partner).wait_recv()

    def nk_own(u):
        @pl.when(top)
        def _():
            own_nk[u].wait()

        @pl.when(row != 0)
        def _():
            nk_arrived(y, u)

        @pl.when(zh != (3 if u == 0 else 1))
        def _():
            nk_send(y, u, at(zh_=zh + (1 if u == 0 else -1)), xsem.at[8 + u])

        nk_send(y, u, at(y_=y + 1), ssem.at[NK])
        nk_send(y, u, at(y_=y - 1), ssem.at[NK])

    def nk_near(u):
        for d in (-1, 1):
            nk_arrived(y + d, u)
            nk_send(y + d, u, at(y_=y - d), ssem.at[NK], half=0 if d < 0 else 1)

    @pl.when(top)
    def _():
        for t in (1, 3, 2):
            for u in range(2):
                src = normals.at[pl.ds(64 * t + 32 * u, 32), :]
                remote(src, nk_part(t, u), xsem.at[10], nk_sem(t, u), (4 * t, col)).start()

    def nr_part(xx, u):
        return nr.at[s, lax.rem(xx + 4, 4), pl.ds(48 * u, 48), :]

    def nr_sem(xx, u):
        return rsem.at[NR, 2 * lax.rem(xx + 4, 4) + u]

    def nr_send(xx, u, device, sem):
        part = nr_part(xx, u)
        remote(part, part, sem, nr_sem(xx, u), device).start()

    def nr_arrived(xx, u):
        part = nr_part(xx, u)
        remote(part, part, ssem.at[NR], nr_sem(xx, u), partner).wait_recv()

    def nr_own(u):
        @pl.when(side)
        def _():
            own_nr[u].wait()

        @pl.when(col != 0)
        def _():
            nr_arrived(x, u)

        @pl.when(zl < 3)
        def _():
            nr_send(x, u, at(zl_=zl + 1), xsem.at[11])

        nr_send(x, u, at(x_=x + 1), ssem.at[NR])
        nr_send(x, u, at(x_=x - 1), ssem.at[NR])

    def nr_near():
        for u in range(2):
            nr_arrived(x - 1, u)
            nr_arrived(x + 1, u)
            if u == 0:
                nr_send(x - 1, 0, at(x_=x + 1), ssem.at[NR])
            else:
                nr_send(x + 1, 1, at(x_=x - 1), ssem.at[NR])

    @pl.when(side)
    def _():
        for t in (2, 6, 1, 3, 7, 4, 5):
            h, q = t % 2, t // 2
            for u in range(2):
                src = normals.at[pl.ds(384 * h + 96 * q + 48 * u, 48), pl.ds(0, B)]
                dst = nr.at[h, q, pl.ds(48 * u, 48), :]
                remote(src, dst, xsem.at[12 + h], rsem.at[NR, 2 * q + u], (row, t)).start()

    def n0_send(q, device, sem):
        part = n0.at[s, q]
        remote(part, part, sem, rsem.at[N0, q], device).start()

    def n0_arrived(q):
        part = n0.at[s, q]
        remote(part, part, ssem.at[N0], rsem.at[N0, q], partner).wait_recv()

    def n0_own(level):
        if level == 0:

            @pl.when(top)
            def _():
                @pl.when(side)
                def _():
                    own_n0.wait()

                @pl.when(col != 0)
                def _():
                    n0_arrived(k)

                for d in (1, 3, 2):
                    n0_send(k, at(y_=y + d), xsem.at[14])
                n0_send(k, at(zh_=zh + 1), xsem.at[15])
                n0_send(k, at(zh_=zh - 1), xsem.at[15])
        elif level == 1:

            @pl.when((zh == 0) & (y != 0))
            def _():
                n0_arrived(k)
                n0_send(k, at(zh_=zh + 1), xsem.at[15])
                n0_send(k, at(zh_=zh - 1), xsem.at[15])
        elif level == 2:

            @pl.when(zh == 1)
            def _():
                n0_arrived(k)
                n0_send(k, at(zh_=zh + 1), xsem.at[16])

            @pl.when(zh == 3)
            def _():
                n0_arrived(k)
        else:

            @pl.when(zh == 2)
            def _():
                n0_arrived(k)

    def n0_plane(d):
        q = slot_of(zl + d, x)
        if d == 0:
            for e in (1, 2, 3):
                n0_send(q, at(zl_=zl + e), ssem.at[N0])
        else:
            n0_arrived(q)
        for e in (1, 3, 2):
            n0_send(q, at(x_=x + e), ssem.at[N0])

    def n0_rest(d):
        for e in (1, 2, 3):
            n0_arrived(slot_of(zl + d, x + e))

    def shared(which, h):
        if which < 4:
            part = dr.at[h, pl.ds(4 * lax.rem(y + which, 4), 4)]
        else:
            part = (d0, n0, nr)[which - 4].at[h]
        return remote(part, part, psem.at[which, 0], psem.at[which, 1], partner)

    def share(which):
        shared(which, s).start()

    far = lax.rem(x - zh + 4, 4) == 2
    off_home = lax.abs(zl - y)

    def only(condition, *steps):
        @pl.when(condition)
        def _():
            for step in steps:
                step[0](*step[1:])

    z_send(DK, design)
    y_send(DK, zh, design)
    own.wait()
    only(source, (to_home,))
    y_near(DK, zh)

    @pl.when(col != 0)
    def _():
        arrived(D0, row)

    @pl.when(side)
    def _():
        own_corner.wait()

    z_send(D0)
    y_send(D0, zh)
    n0_own(0)
    only(zh == 0, (nk_own, 0), (nk_own, 1))
    only(zl == 0, (nr_own, 0), (nr_own, 1))
    z_near(DK, -1)
    z_near(DK, 1)
    n0_own(1)
    only(zl == 1, (nr_own, 0), (nr_own, 1))
    y_near(DK, zh - 1)
    y_near(DK, zh + 1)
    only((zh != x) & (lax.rem(x - zh + 4, 4) != 2), (to_home,))
    z_near(D0, -1)
    z_near(D0, 1)
    n0_own(2)
    only(zh == 1, (nk_own, 0))
    only(zh == 3, (nk_own, 1))
    only(zl == 2, (nr_own, 0), (nr_own, 1))
    z_far(DK)
    only(far, (to_home,))
    z_far(D0)
    n0_own(3)
    n0_plane(0)
    only(zl == 3, (nr_own, 0), (nr_own, 1))
    only(zh == 2, (nk_own, 0), (nk_own, 1))
    y_near(DK, zh + 2)
    only(off_home == 0, *[(along, d) for d in (0, 1, 3, 2)])
    for d in (1, 3, 2):
        n0_plane(d)
    for zz in (0, -1, 1, 2):
        y_far(D0, zh + zz)
    share(4)
    only(zh == 3, (nk_own, 0))
    only(zh == 1, (nk_own, 1))
    nr_near()
    only(off_home == 1, *[(along, d) for d in (0, 1, 3, 2)])
    for d in (0, 1, 3, 2):
        n0_rest(d)
    share(5)
    nk_near(0)
    nk_near(1)
    shared(4, 1 - s).wait_recv()

    def nr_far():
        nr_arrived(x + 2, 0)
        nr_arrived(x + 2, 1)
        share(6)

    def nk_far():
        nk_arrived(y + 2, 0)
        nk_arrived(y + 2, 1)

    def x_last(d):
        x_far(d)
        share(d)

    steps = [(lambda: only(off_home == 2, *[(along, d) for d in (0, 1, 3, 2)]))]
    steps += [nr_far, (lambda: only(off_home == 3, *[(along, d) for d in (0, 1, 3, 2)]))]
    steps += [functools.partial(x_near, d) for d in (0, 1, 3, 2)]
    steps += [nk_far] + [functools.partial(x_last, d) for d in (0, 1, 3, 2)]
    turn = [0]

    def tick():
        turn[0] += 1
        if turn[0] % 2 == 0 and steps:
            steps.pop(0)()

    rows, cols = tile.shape
    half = rows // 2
    toeplitz[...] = jnp.zeros_like(toeplitz)
    for i in range(4):
        here = slice(P_SIZE * i, P_SIZE * (i + 1))
        toeplitz[here, P_SIZE * i : P_SIZE * (i + 1)] = filters[1]
        toeplitz[here, P_SIZE * (i + 1) : P_SIZE * (i + 2)] = filters[0]

    def filtered(load, dst):
        width = dst.shape[1]
        for q in range(0, 16, 4):
            first = max(q - 1, 0)
            data = load(first, q + 4).reshape(P_SIZE * (q + 4 - first), width)
            taps = toeplitz[:, P_SIZE:] if q == 0 else toeplitz[...]
            dst[P_SIZE * q : P_SIZE * (q + 4), :] = dot(taps, data)

    filtered(lambda a, b: jnp.concatenate([d0[0, a:b], d0[1, a:b]], axis=2), f0)
    gram = dot(f0[...], f0[...], 0, 0)
    steps.pop(0)()
    for zz in (0, -1, 1, 2):
        y_far(DK, zh + zz)
    filtered(lambda a, b: dk[a:b], fk)
    shared(5, 1 - s).wait_recv()
    reg0 = jnp.where(iota((B, B), 0) == iota((B, B), 1), regular[:, :B], 0.0)
    corner[...] = n0[...].reshape(B, B) + gram + reg0
    inverse_factor(corner, inverse, B, 128, tick)
    while steps:
        steps.pop(0)()
    w = inverse[...]
    f0s = split(f0[...])
    fks = split(fk[...])
    reg = regular[:, pl.ds(pl.multiple_of(cols * col, 128), cols)]
    same = iota((B, cols), 0) == iota((B, cols), 1) + cols * col
    pks = split(dot(w, nk[...] + dot3(f0s, fks) + jnp.where(same, reg, 0.0)))
    own_tile.wait()
    shared(6, 1 - s).wait_recv()
    flush = []
    for e in range(2):
        h = s if e == 0 else 1 - s
        if e == 1:
            for which in range(4):
                shared(which, h).wait_recv()
        filtered(lambda a, b: dr[h, a:b], fr)
        frs = split(fr[...])
        first = row * rows + half * h
        same = iota((half, B), 0) + first == iota((half, B), 1)
        strip = nr[h].reshape(half, B) + dot3(frs, f0s) + jnp.where(same, regular[:, :B], 0.0)
        pr = dot(strip, w, 1, 1)
        here = pl.ds(pl.multiple_of(half * h, 8), half)
        same = iota((half, cols), 0) + first == iota((half, cols), 1) + cols * col
        value = tile[here, :] + jnp.where(same, reg, 0.0) + dot3(frs, fks)
        result[e] = value - dot3(split(pr), pks, 1, 0)

        @pl.when(side)
        def _():
            result[e, :, :B] = pr

        flush.append(copy(result.at[e], out.at[here, :], 10 + e))
        flush[e].start()

    for which in range(7):
        shared(which, s).wait_send()

    def drained(part, flow):
        remote(part, part, ssem.at[flow], rsem.at[DK, 0], partner).wait_send()

    drained(dk.at[pl.ds(0, 15)], DK)
    drained(d0.at[0, pl.ds(0, 15)], D0)
    drained(dr.at[0, pl.ds(0, 12)], DR)
    drained(nk.at[pl.ds(0, 192), :], NK)
    drained(nr.at[0, pl.ds(0, 3)], NR)
    drained(n0.at[0, pl.ds(0, 15)], N0)

    @pl.when(side)
    def _():
        sent(d0.at[0, pl.ds(0, 15)], 0)
        sent(d0.at[1], 1)
        sent(nr.at[0, pl.ds(0, 3)], 12)
        sent(nr.at[1], 13)

    @pl.when(top & side)
    def _():
        sent(n0.at[0, pl.ds(0, 15)], 2)
        sent(n0.at[1], 3)

    @pl.when(source)
    def _():
        sent(dk.at[pl.ds(0, 3)], 4)

    @pl.when(zl != y)
    def _():
        sent(hop, 5)

    @pl.when(up)
    def _():
        sent(dk.at[pl.ds(0, 4)], 6)

    @pl.when(down)
    def _():
        sent(dk.at[pl.ds(0, 4)], 7)

    @pl.when(zh != 3)
    def _():
        sent(nk_part(0, 0), 8)

    @pl.when(zh != 1)
    def _():
        sent(nk_part(0, 0), 9)

    @pl.when(top)
    def _():
        sent(nk.at[pl.ds(0, 192), :], 10)
        sent(n0.at[0, pl.ds(0, 3)], 14)

    @pl.when(zl < 3)
    def _():
        sent(nr.at[0, 0], 11)

    @pl.when(zh == 0)
    def _():
        sent(n0.at[0, pl.ds(0, 2)], 15)

    @pl.when(zh == 1)
    def _():
        sent(n0.at[0, 0], 16)

    flush[0].wait()
    flush[1].wait()


def local_step(normals, design, filters, regular):
    f32 = jnp.float32
    rows, cols = normals.shape
    dma = pltpu.SemaphoreType.DMA
    blocks = [(16, P_SIZE, cols), (2, 16, P_SIZE, cols), (2, 16, P_SIZE, 128), (B, cols), (2, 4, 96, B), (2, 16, 8, B)]
    blocks += [(P_SIZE, cols)]
    sems = [dma((6,)), dma((7, 16)), dma((17,)), dma((7, 2)), dma((12,))]
    work = [(rows, cols), (2, rows // 2, cols), (4 * P_SIZE, 5 * P_SIZE), (OBS, B), (OBS, cols), (OBS, cols), (B, B), (B, B)]
    return pl.pallas_call(
        kernel,
        out_shape=jax.ShapeDtypeStruct((rows, cols), f32),
        in_specs=[pl.BlockSpec(memory_space=space) for space in (VMEM, pl.ANY, VMEM, VMEM)],
        out_specs=pl.BlockSpec(memory_space=pl.ANY),
        scratch_shapes=[VMEM(shape, f32) for shape in blocks] + sems + [VMEM(shape, f32) for shape in work],
        compiler_params=pltpu.CompilerParams(collective_id=0, has_side_effects=True),
    )(design, normals, filters, regular.reshape(1, -1))


def dot(a, b, da=1, db=0, precision=HIGHEST):
    return lax.dot_general(a, b, (((da,), (db,)), ((), ())), precision=precision, preferred_element_type=jnp.float32)


def split(a):
    high = a.astype(jnp.bfloat16)
    return high, (a - high.astype(jnp.float32)).astype(jnp.bfloat16)


def dot3(a, b, da=0, db=0):
    (ah, al), (bh, bl) = a, b
    return dot(ah, bh, da, db, None) + (dot(ah, bl, da, db, None) + dot(al, bh, da, db, None))


def iota(shape, dim):
    return lax.broadcasted_iota(jnp.int32, shape, dim)


def eliminate(block, tick):
    nb = block.shape[0]
    wide = (8, 2 * nb)
    right = (iota((nb, nb), 0) == iota((nb, nb), 1)).astype(jnp.float32)
    rows = [jnp.concatenate([block[o : o + 8, :], right[o : o + 8, :]], axis=1) for o in range(0, nb, 8)]
    place = iota(wide, 0)
    done = []
    for g in range(nb // 8):
        t = 8 * g
        below = range(g + 1, nb // 8)
        lead = [jnp.broadcast_to(rows[g][j : j + 1, :], wide) for j in range(8)]
        pivots = {
            (j, c): jnp.broadcast_to(lead[j][:, t + c : t + c + 1], wide) for j in range(8) for c in range(j, 8)
        }
        weights = {(i, j): jnp.broadcast_to(rows[i][:, t + j : t + j + 1], wide) for i in below for j in range(8)}
        final = jnp.zeros(wide, jnp.float32)
        diag = jnp.ones(wide, jnp.float32)
        for j in range(8):
            inverse = 1.0 / pivots[j, j]
            for c in range(j + 1, 8):
                ratio = pivots[j, c] * inverse
                for d in range(c, 8):
                    pivots[c, d] = pivots[c, d] - ratio * pivots[j, d]
                lead[c] = lead[c] - ratio * lead[j]
                for i in below:
                    weights[i, c] = weights[i, c] - ratio * weights[i, j]
            scaled = lead[j] * inverse
            for i in below:
                rows[i] = rows[i] - weights[i, j] * scaled
            final = jnp.where(place == j, lead[j], final)
            diag = jnp.where(place == j, pivots[j, j], diag)
        done.append((final * (1.0 / jnp.sqrt(diag)))[:, nb:])
        tick()
    return jnp.concatenate(done, axis=0)


def inverse_factor(a, w, n, nb, tick):
    w[...] = (iota((n, n), 0) == iota((n, n), 1)).astype(jnp.float32)
    for o in range(0, n, nb):
        e = o + nb
        own = eliminate(a[o:e, o:e], tick)
        left = dot(own, w[o:e, :e])
        w[o:e, :e] = left
        if e < n:
            right = dot(own, a[o:e, e:])
            a[e:, e:] -= dot(right, right, 0, 0)
            w[e:, :e] -= dot(right, left, 0, 0)


def body(normals, design, filter_blocks, regular):
    return local_step(normals, design, filter_blocks, regular)


def solution(mesh):
    in_specs = (P("row", "col"), P("row", "col"), P(), P())
    out_specs = P("row", "col")
    return jax.shard_map(body, mesh=mesh, in_specs=in_specs, out_specs=out_specs, check_vma=False)
```
